32 devices in a mesh: dp: 8 (over y, x, core), mp: 4 (over z).
Axes of the slice: x: 2, y: 2, z: 4, core: 2. Of those that a mesh axis runs over, the one named last changes fastest.
Arguments:
- activations: bfloat16 [1024, 2560], P('dp'), may hold values from -6 to 6
- grad_hidden: bfloat16 [1024, 8192], P('dp', 'mp'), may hold values from -0.059814453 to 0.059814453
- up_weight: bfloat16 [2560, 8192], P('dp', 'mp'), may hold values from -6 to 6
- error_feedback: bfloat16 [8, 2560, 8192], P('dp', None, 'mp'), may hold values from -0.75 to 0.75
- query_previous: float32 [8192, 128], P('mp'), may hold values from -6 to 6
Outputs:
- grad_input: bfloat16 [1024, 2560], P('dp', 'mp')
- error_next: bfloat16 [8, 2560, 8192], P('dp', None, 'mp')
- update: float32 [2560, 8192], P('dp', 'mp')
- query_next: float32 [8192, 128], P('mp')
The draws below stay inside these ranges and needn't reach their ends.
All inputs are finite; a program needn't handle non-finite values.
Results may differ from the reference program's by a relative error of at most 0.0005.
Values may be sent and summed in bfloat16 or wider, within the bound.
A program may use at most 128 MiB of HBM per device.

```python
import jax
import jax.numpy as jnp
from jax import lax

D = 2560
FF = 8192
R = 128
TOK_DEV = 128
TOKENS = 1024
N_DP = 8


def with_spikes(drawn, key, source, target, blocks, factor):
    def block_of(position):
        return (jnp.arange(drawn.shape[position]) // (drawn.shape[position] // blocks)).reshape((-1,) + (1,) * (drawn.ndim - 1 - position))

    near = jax.random.permutation(key, blocks)[block_of(target)]
    second = (block_of(target) + blocks // 2) % blocks
    return jnp.where((block_of(source) == near) | (block_of(source) == second), factor * drawn, drawn)


def level_of(rng, dims, split, smallest, largest):
    gain = 1.0
    for axis_at, blocks in split:
        draws = jax.random.uniform(jax.random.fold_in(jax.random.fold_in(rng, 6), axis_at), (blocks,), jnp.float32, smallest / len(split), largest / len(split))
        gain = gain * jnp.repeat(jnp.exp(draws), dims[axis_at] // blocks).reshape((-1,) + (1,) * (len(dims) - 1 - axis_at))
    return gain


def scatter_about(stream_key, extent, deviation, reach, split=(), kind=jnp.bfloat16):
    entries = jax.random.normal(stream_key, extent, jnp.float32) * deviation
    if len(split) > 0:
        entries = level_of(stream_key, extent, split, -0.22, 0.18) * entries
    return jnp.clip(entries, min=-reach, max=reach).astype(kind)


def noise_with(own_key, dims, scale, limit, shards, heavy, kind=jnp.bfloat16):
    result = scale * jax.random.normal(own_key, dims, jnp.float32)
    if shards:
        result = result * level_of(own_key, dims, shards, -0.22, 0.18)
    return jnp.clip(with_spikes(result, jax.random.fold_in(own_key, 3), *heavy), -limit, limit).astype(kind)


def setup_inputs(seed: int = 0) -> dict:
    arg_keys = jax.random.split(jax.random.key(seed), 6)
    return {
        "activations": noise_with(arg_keys[0], (TOKENS, D), 1.0, 6.0, ((0, 8),), (0, 1, 8, 2.0)),
        "grad_hidden": scatter_about(arg_keys[1], (TOKENS, FF), 0.01, 0.059814453, ((0, 8), (1, 4))),
        "up_weight": scatter_about(arg_keys[2], (D, FF), 1.0, 6.0, ((0, 8), (1, 4))),
        "error_feedback": scatter_about(arg_keys[3], (N_DP, D, FF), 0.125, 0.75, ((0, 8), (2, 4))),
        "query_previous": scatter_about(arg_keys[4], (FF, R), 1.0, 6.0, ((0, 4),), jnp.float32),
    }


HIGHEST = lax.Precision.HIGHEST

def merged_of(error_block, acts_block, hidden_block):
    return error_block.astype(jnp.float32) + jnp.dot(acts_block.T.astype(jnp.float32), hidden_block.astype(jnp.float32), preferred_element_type=jnp.float32)

def reference(activations, grad_hidden, up_weight, error_feedback, query_previous):
    grad_input = jnp.dot(grad_hidden.astype(jnp.float32), up_weight.T.astype(jnp.float32), preferred_element_type=jnp.float32).astype(jnp.bfloat16)
    acts_split = activations.reshape(N_DP, TOK_DEV, D)
    hidden_split = grad_hidden.reshape(N_DP, TOK_DEV, FF)
    stacked = (error_feedback, acts_split, hidden_split)

    def add_project(running, inputs):
        merged = merged_of(inputs[0], inputs[1], inputs[2])
        return (running + jnp.dot(merged.astype(jnp.float32), query_previous.astype(jnp.float32), precision=HIGHEST, preferred_element_type=jnp.float32), None)
    project, unused = lax.scan(add_project, jnp.zeros((D, R), jnp.float32), stacked)
    gram_matrix = jnp.dot(project.T.astype(jnp.float32), project.astype(jnp.float32), precision=HIGHEST, preferred_element_type=jnp.float32)
    factor = jnp.linalg.cholesky(gram_matrix)
    basis = lax.linalg.triangular_solve(factor, project, left_side=False, lower=True, transpose_a=True)

    def add_query(running, inputs):
        merged = merged_of(inputs[0], inputs[1], inputs[2])
        return (running + jnp.dot(merged.T.astype(jnp.float32), basis.astype(jnp.float32), precision=HIGHEST, preferred_element_type=jnp.float32), None)
    query_total, unused = lax.scan(add_query, jnp.zeros((FF, R), jnp.float32), stacked)
    query_next = query_total / N_DP
    update = jnp.dot(basis.astype(jnp.float32), query_next.T.astype(jnp.float32), precision=HIGHEST, preferred_element_type=jnp.float32)

    def residual_of(inputs):
        return (merged_of(inputs[0], inputs[1], inputs[2]) - update).astype(jnp.bfloat16)
    error_next = lax.map(residual_of, stacked)
    return (grad_input, error_next, update, query_next)
```

```python
import functools

import jax
import jax.numpy as jnp
from jax import lax
from jax.experimental import pallas as pl
from jax.experimental.pallas import tpu as pltpu
from jax.sharding import PartitionSpec as P

HIGHEST = lax.Precision.HIGHEST
MESH = pl.DeviceIdType.MESH
F32 = jnp.float32
BF16 = jnp.bfloat16
CORES = 2
PANEL = 16
PIECES = 2


def split(x):
    high = x.astype(BF16)
    return high, (x - high.astype(F32)).astype(BF16)


def dot(a, b, da=1, db=0, precision=None):
    return lax.dot_general(
        a, b, (((da,), (db,)), ((), ())), precision=precision, preferred_element_type=F32
    )


def halves(x):
    r = x.shape[1] // 2
    return x[:, :r] + x[:, r:]


def flip(v, r):
    out, bit = v, 1
    while bit <= r:
        if r & bit:
            out = out + bit - 2 * bit * lax.rem(v // bit, 2)
        bit *= 2
    return out


def inverse_factor(gram, aug):
    r = gram.shape[0]
    rows = lax.broadcasted_iota(jnp.int32, (r, r), 0)
    cols = lax.broadcasted_iota(jnp.int32, (r, r), 1)
    aug[:, :r] = gram
    aug[:, r:] = jnp.where(rows == cols, 1.0, 0.0).astype(F32)
    prow = lax.broadcasted_iota(jnp.int32, (PANEL, 2 * r), 0)
    for start in range(0, r, PANEL):
        panel = aug[start : start + PANEL, :]
        for t in range(PANEL):
            j = start + t
            scale = lax.rsqrt(panel[t : t + 1, j : j + 1])
            row = panel[t : t + 1, :] * scale
            col = panel[:, j : j + 1] * scale
            panel = jnp.where(
                prow == t, row, jnp.where(prow > t, panel - col * row, panel)
            )
        aug[start : start + PANEL, :] = panel
        rest = start + PANEL
        if rest < r:
            change = dot(panel[:, :r], panel, 0, 0, HIGHEST)
            aug[rest:, :] = aug[rest:, :] - change[rest:, :]
    return aug[:, r:]


def compress(
    n_dp, n_mp, e_hbm, a_hbm, h_hbm, w_hbm, q_hbm, qn_ref, x_ref, g_ref,
    e, a, hall, w, q, q2, p, p2, pt2, tacc, aug, acc, zin, zfin, csend, crecv, xsend, xrecv,
    t, tcrecv, txsend, txrecv, part, zrecv, gsend, grecv,
    l_s, c_s, c_r, x_s, x_r, z_s, z_r, gz_s, gz_r, gx_s, gx_r, gc_s, gc_r,
    tc_s, tc_r, tx_s, tx_r, qx_s, qx_r, qc_s, qc_r, h_s, h_r, w_s, w_r, pz_s, pz_r, gg_s, gg_r,
):
    chips = n_dp // CORES
    me, mp = lax.axis_index("dp"), lax.axis_index("mp")
    chip, core = me // CORES, lax.rem(me, CORES)
    other = 1 - core
    partner = (chip * CORES + other, mp)
    d, rank = p.shape
    ff = t.shape[0]
    tok = a.shape[0]
    pr, tr, tq = d // n_dp, ff // n_dp, tok // n_mp
    wide = CORES * pr
    zr = pr // n_mp if pr % (8 * n_mp) == 0 else pr
    n_sub = chips // n_mp
    goal = chip // n_sub

    def chip_at(r):
        return flip(chip, r)

    def same_core(r):
        return (chip_at(r) * CORES + core, mp)

    def along(r):
        return (me, flip(mp, r))

    def rows(i, n, unit=8):
        return pl.ds(pl.multiple_of(i * n, unit), n)

    def send(src, dst, s, r, to):
        return pltpu.make_async_remote_copy(
            src_ref=src, dst_ref=dst, send_sem=s, recv_sem=r, device_id=to, device_id_type=MESH
        )

    barrier = pltpu.get_barrier_semaphore()
    pl.semaphore_signal(barrier, inc=1, device_id=partner, device_id_type=MESH)
    for r in range(1, chips):
        pl.semaphore_signal(barrier, inc=1, device_id=same_core(r), device_id_type=MESH)
    for r in range(1, n_mp):
        pl.semaphore_signal(barrier, inc=1, device_id=along(r), device_id_type=MESH)
    for s in range(n_sub):
        for q_at in range(n_mp):
            source = mp * n_sub + s

            @pl.when(jnp.logical_or(source != chip, q_at != mp))
            def _():
                pl.semaphore_signal(
                    barrier, inc=1, device_id=(source * CORES + core, q_at), device_id_type=MESH
                )

    loads = []

    def load(src, dst):
        copy = pltpu.make_async_copy(src, dst, l_s.at[len(loads)])
        copy.start()
        loads.append(copy)
        return copy

    h_load = load(h_hbm, hall.at[0])
    q_load = load(q_hbm, q)
    a_load = load(a_hbm, a)
    order = [chip_at(r) * CORES + other for r in range(1, chips)] + [partner[0]]
    order += [chip_at(r) * CORES + core for r in range(1, chips)] + [me]
    e_loads = [load(e_hbm.at[rows(b, pr, 16), :], e.at[rows(b, pr, 16), :]) for b in order]
    w_load = load(w_hbm, w.at[rows(core, pr, 16), :])

    pl.semaphore_wait(barrier, 1 + (chips - 1) + (n_mp - 1) + chips - jnp.where(goal == mp, 1, 0))

    tp = tok // PIECES
    h_copies = {}

    def send_hidden(r, k):
        at = pl.ds(k * tp, tp)
        i = r * PIECES + k
        copy = send(h_hbm.at[at, :], hall.at[r, at, :], h_s.at[i], h_r.at[i], same_core(r))
        copy.start()
        h_copies[r, k] = copy

    near = [r for r in range(1, chips) if r & (r - 1) == 0]
    far = [r for r in range(1, chips) if r & (r - 1) != 0]
    for r in near:
        send_hidden(r, 0)
    w_copy = send(w_hbm, w.at[rows(core, pr, 16), :], w_s.at[0], w_r.at[0], partner)
    w_copy.start()

    h_load.wait()
    q_load.wait()
    q_high, q_low = split(q[...])
    q2[:, :rank] = q_high
    q2[:, rank:] = q_low
    hq = halves(dot(hall[0], q2[...]))
    hq2 = jnp.concatenate(split(hq), axis=1)
    a_load.wait()
    p[...] = halves(dot(a[...], hq2, 0, 0))

    def project(i):
        e_loads[i].wait()
        at = rows(order[i], pr, 16)
        return halves(dot(e[at, :], q2[...])) + p[at, :]

    core_copies = []
    for i in range(chips):
        csend[i] = project(i)
        copy = send(csend.at[i], crecv.at[i], c_s.at[i], c_r.at[i], partner)
        copy.start()
        core_copies.append(copy)
    x_copies = []
    for i in range(chips):
        value = project(chips + i)
        core_copies[i].wait_recv()
        value = value + crecv[i]
        if i < chips - 1:
            xsend[i] = value
            copy = send(xsend.at[i], xrecv.at[i], x_s.at[i], x_r.at[i], same_core(i + 1))
            copy.start()
            x_copies.append(copy)
        else:
            acc[...] = value

    z_parts = {}

    def partial_input(r):
        part[r] = dot(hall[r], w[...], 1, 1)

    def send_partial(r):
        for s in range(1, n_mp):
            i = r * n_mp + s
            copy = send(
                part.at[r, rows(flip(mp, s), tq), :], zrecv.at[r, s - 1],
                pz_s.at[i], pz_r.at[i], along(s),
            )
            copy.start()
            z_parts[r, s] = copy

    w_load.wait()
    w_copy.wait_recv()
    partial_input(0)
    send_partial(0)

    value = acc[...]
    for i, copy in enumerate(x_copies):
        copy.wait_recv()
        value = value + xrecv[i]
    acc[...] = value
    for r in near:
        for k in range(1, PIECES):
            send_hidden(r, k)

    def segment(i):
        return rows(i, zr) if zr < pr else pl.ds(0, pr)

    z_copies = []
    for r in range(1, n_mp):
        copy = send(
            acc.at[segment(flip(mp, r)), :], zin.at[r - 1], z_s.at[r - 1], z_r.at[r - 1], along(r)
        )
        copy.start()
        z_copies.append(copy)
    value = acc[segment(mp), :]
    for r in far:
        for k in range(PIECES):
            send_hidden(r, k)
    for i, copy in enumerate(z_copies):
        copy.wait_recv()
        value = value + zin[i]
    if zr < pr:
        zfin[...] = value
        here = pl.ds(pl.multiple_of(me * pr + mp * zr, 8), zr)
        p[here, :] = value
        gz = []
        for r in range(1, n_mp):
            copy = send(zfin, p.at[here, :], gz_s.at[r - 1], gz_r.at[r - 1], along(r))
            copy.start()
            gz.append(copy)
        for copy in gz:
            copy.wait_recv()
        z_copies += gz
    else:
        p[rows(me, pr), :] = value

    class Gather:
        def __init__(self, ref, n, x_s, x_r, c_s, c_r):
            self.ref, self.n = ref, n
            self.x_s, self.x_r, self.c_s, self.c_r = x_s, x_r, c_s, c_r
            own = rows(me, n)
            self.across, self.down = {}, {}
            for r in range(1, chips):
                copy = send(ref.at[own, :], ref.at[own, :], x_s.at[r], x_r.at[r], same_core(r))
                copy.start()
                self.across[r] = copy
            self.forward(0)

        def forward(self, r):
            if r:
                self.across[r].wait_recv()
            at = rows(chip_at(r) * CORES + core, self.n)
            copy = send(self.ref.at[at, :], self.ref.at[at, :], self.c_s.at[r], self.c_r.at[r], partner)
            copy.start()
            self.down[r] = copy

        def finish(self):
            for copy in list(self.across.values()) + list(self.down.values()):
                copy.wait_send()

    for copy in core_copies + x_copies + z_copies:
        copy.wait_send()
    gather = Gather(p, pr, gx_s, gx_r, gc_s, gc_r)

    for r in near:
        for k in range(PIECES):
            h_copies[r, k].wait_recv()
        partial_input(r)
        send_partial(r)

    width = 256

    def accumulate(r, gram):
        gather.down[r].wait_recv()
        at = pl.ds(pl.multiple_of(chip_at(r) * wide, 16), wide)
        block = p[at, :]
        high, low = split(block)
        p2[at, :rank] = high
        p2[at, rank:] = low
        turned = block.T
        high, low = split(turned)
        pt2[:rank, :] = high
        pt2[rank:, :] = low
        last = r == chips - 1
        if last:
            ap = halves(dot(a[...], p2[...])).T
            ap2 = jnp.concatenate(split(ap), axis=0)

        def term(n, carry):
            cols = pl.ds(pl.multiple_of(n * width, width), width)
            both = dot(pt2[...], e[at, cols])
            total = both[:rank] + both[rank:]
            if r:
                total = total + tacc[:, cols]
            if last:
                both = dot(ap2, hall[0, :, cols])
                t[cols, :] = (total + (both[:rank] + both[rank:])).T
            else:
                tacc[:, cols] = total
            return carry

        lax.fori_loop(0, ff // width, term, 0)
        return lambda: gram + dot(turned, block, 1, 0, HIGHEST)

    gram = accumulate(0, 0.0)()
    for r in near:
        gather.forward(r)
    for r in range(1, chips - 1):
        if r in far:
            gather.forward(r)
        gram = accumulate(r, gram)()
    gather.forward(chips - 1)
    add_gram = accumulate(chips - 1, gram)

    t_copies = []
    for i in range(chips):
        block = chip_at((i + 1) % chips) * CORES + other
        copy = send(t.at[rows(block, tr), :], tcrecv.at[i], tc_s.at[i], tc_r.at[i], partner)
        copy.start()
        t_copies.append(copy)
    gram = add_gram()
    tx_copies = []
    for i in range(chips):
        t_copies[i].wait_recv()
        value = t[rows(chip_at((i + 1) % chips) * CORES + core, tr), :] + tcrecv[i]
        txsend[i] = value
        if i < chips - 1:
            copy = send(txsend.at[i], txrecv.at[i], tx_s.at[i], tx_r.at[i], same_core(i + 1))
            copy.start()
            tx_copies.append(copy)
    for r in far:
        for k in range(PIECES):
            h_copies[r, k].wait_recv()
        partial_input(r)
        send_partial(r)
    inverse = inverse_factor(gram, aug)
    value = txsend[chips - 1]
    for i, copy in enumerate(tx_copies):
        copy.wait_recv()
        value = value + txrecv[i]
    qn_ref[rows(me, tr), :] = dot(value, inverse, 1, 1, HIGHEST) / n_dp
    gather.finish()
    gather = Gather(qn_ref, tr, qx_s, qx_r, qc_s, qc_r)

    g_copies = []
    for r in range(chips):
        value = part[r, rows(mp, tq), :]
        for s in range(1, n_mp):
            z_parts[r, s].wait_recv()
            value = value + zrecv[r, s - 1]
        gsend[r] = value.astype(BF16)
        place = grecv.at[lax.rem(chip, n_sub), rows(mp, tq, 16), :]
        slot = lax.rem(chip, n_sub) * n_mp + mp
        to = (chip_at(r) * CORES + core, goal)
        copy = send(gsend.at[r], place, gg_s.at[r], gg_r.at[slot], to)
        if r:
            copy.start()
        else:

            @pl.when(goal != mp)
            def _():
                copy.start()

            @pl.when(goal == mp)
            def _():
                place[...] = gsend[0]

        g_copies.append(copy)

    high, low = split(dot(p[...], aug[:, rank:], 1, 1, HIGHEST))
    x_ref[:, :rank] = high
    x_ref[:, rank : 2 * rank] = low
    x_ref[:, 2 * rank : 3 * rank] = high
    x_ref[:, 3 * rank :] = a[...].T

    for r in range(1, chips):
        gather.forward(r)
    for s in range(n_sub):
        for q_at in range(n_mp):
            at = pl.ds(q_at * tq, tq)
            arrival = send(
                gsend.at[0], grecv.at[s, at, :], gg_s.at[0], gg_r.at[s * n_mp + q_at], partner
            )

            @pl.when(jnp.logical_or(mp * n_sub + s != chip, q_at != mp))
            def _():
                arrival.wait_recv()

        g_ref[:, s * wide : (s + 1) * wide] = grecv[s]
    for copy in gather.down.values():
        copy.wait_recv()
    gather.finish()
    for copy in t_copies + tx_copies + list(h_copies.values()) + list(z_parts.values()) + [w_copy]:
        copy.wait_send()
    for r in range(1, chips):
        g_copies[r].wait_send()

    @pl.when(goal != mp)
    def _():
        g_copies[0].wait_send()


def residual(n_dp, e_ref, h_ref, qn_ref, x_ref, g_ref, out_ref, up_ref, q_out, g_out, y):
    rank = qn_ref.shape[1]
    d = e_ref.shape[0]
    high, low = split(-qn_ref[...].T)
    y[:rank] = high
    y[rank : 2 * rank] = high
    y[2 * rank : 3 * rank] = low
    y[3 * rank :] = h_ref[...]
    q_out[...] = qn_ref[...]

    @pl.when(pl.program_id(0) == 0)
    def _():
        g_out[...] = g_ref[...]

    share = up_ref.shape[0]
    own = pl.ds(pl.multiple_of(lax.axis_index("dp") * share, 16), share)
    up_ref[...] = -dot(x_ref[own, : 3 * rank], y[: 3 * rank, :])
    block = d // 4
    for i in range(4):
        at = slice(i * block, (i + 1) * block)
        out_ref[at, :] = (e_ref[at, :].astype(F32) + dot(x_ref[at, :], y[...])).astype(BF16)


def local(n_dp, n_mp, activations, grad_hidden, up_weight, error_feedback, query_previous):
    error = error_feedback[0]
    d, ff = error.shape
    tok, rank = activations.shape[0], query_previous.shape[1]
    chips = n_dp // CORES
    pr, tr, tq = d // n_dp, ff // n_dp, tok // n_mp
    wide = CORES * pr
    zr = pr // n_mp if pr % (8 * n_mp) == 0 else pr
    n_sub = chips // n_mp
    vmem = pl.BlockSpec(memory_space=pltpu.VMEM)
    hbm = pl.BlockSpec(memory_space=pl.ANY)
    dma = pltpu.SemaphoreType.DMA
    pairs = lambda n: [dma((n,)), dma((n,))]
    query_next, factors, grad_input = pl.pallas_call(
        functools.partial(compress, n_dp, n_mp),
        out_shape=(
            jax.ShapeDtypeStruct((ff, rank), F32),
            jax.ShapeDtypeStruct((d, 3 * rank + tok), BF16),
            jax.ShapeDtypeStruct((tok, d // n_mp), BF16),
        ),
        in_specs=[hbm, hbm, hbm, hbm, hbm],
        out_specs=(vmem, vmem, vmem),
        scratch_shapes=[
            pltpu.VMEM((d, ff), BF16),
            pltpu.VMEM((tok, d), BF16),
            pltpu.VMEM((chips, tok, ff), BF16),
            pltpu.VMEM((wide, ff), BF16),
            pltpu.VMEM((ff, rank), F32),
            pltpu.VMEM((ff, 2 * rank), BF16),
            pltpu.VMEM((d, rank), F32),
            pltpu.VMEM((d, 2 * rank), BF16),
            pltpu.VMEM((2 * rank, wide), BF16),
            pltpu.VMEM((rank, ff), F32),
            pltpu.VMEM((rank, 2 * rank), F32),
            pltpu.VMEM((pr, rank), F32),
            pltpu.VMEM((n_mp, zr, rank), F32),
            pltpu.VMEM((zr, rank), F32),
            pltpu.VMEM((chips, pr, rank), F32),
            pltpu.VMEM((chips, pr, rank), F32),
            pltpu.VMEM((chips, pr, rank), F32),
            pltpu.VMEM((chips, pr, rank), F32),
            pltpu.VMEM((ff, rank), F32),
            pltpu.VMEM((chips, tr, rank), F32),
            pltpu.VMEM((chips, tr, rank), F32),
            pltpu.VMEM((chips, tr, rank), F32),
            pltpu.VMEM((chips, tok, wide), F32),
            pltpu.VMEM((chips, n_mp - 1, tq, wide), F32),
            pltpu.VMEM((chips, tq, wide), BF16),
            pltpu.VMEM((n_sub, tok, wide), BF16),
            dma((n_dp + 4,)),
        ]
        + pairs(chips) + pairs(chips) + pairs(n_mp) + pairs(n_mp) + pairs(chips) + pairs(chips)
        + pairs(chips) + pairs(chips) + pairs(chips) + pairs(chips)
        + pairs(PIECES * chips) + pairs(1) + pairs(chips * n_mp) + pairs(chips),
        compiler_params=pltpu.CompilerParams(
            collective_id=0, has_side_effects=True, vmem_limit_bytes=54 << 20
        ),
        cost_estimate=pl.CostEstimate(flops=64 * d * ff * rank, bytes_accessed=48 * d * ff, transcendentals=0),
        name="compress",
    )(error, activations, grad_hidden, up_weight, query_previous)

    width = 256
    error_next, update, query_out, grad_out = pl.pallas_call(
        functools.partial(residual, n_dp),
        out_shape=(
            jax.ShapeDtypeStruct((d, ff), BF16),
            jax.ShapeDtypeStruct((pr, ff), F32),
            jax.ShapeDtypeStruct((ff, rank), F32),
            jax.ShapeDtypeStruct((tok, d // n_mp), BF16),
        ),
        grid=(ff // width,),
        in_specs=[
            pl.BlockSpec((d, width), lambda i: (0, i)),
            pl.BlockSpec((tok, width), lambda i: (0, i)),
            pl.BlockSpec((width, rank), lambda i: (i, 0)),
            pl.BlockSpec((d, 3 * rank + tok), lambda i: (0, 0)),
            pl.BlockSpec((tok, d // n_mp), lambda i: (0, 0)),
        ],
        out_specs=(
            pl.BlockSpec((d, width), lambda i: (0, i)),
            pl.BlockSpec((pr, width), lambda i: (0, i)),
            pl.BlockSpec((width, rank), lambda i: (i, 0)),
            pl.BlockSpec((tok, d // n_mp), lambda i: (0, 0)),
        ),
        scratch_shapes=[pltpu.VMEM((3 * rank + tok, width), BF16)],
        compiler_params=pltpu.CompilerParams(vmem_limit_bytes=54 << 20),
        cost_estimate=pl.CostEstimate(flops=8 * d * ff * rank, bytes_accessed=4 * d * ff, transcendentals=0),
        name="residual",
    )(error, grad_hidden, query_next, factors, grad_input)
    return grad_out, error_next[None], update, query_out


def solution(mesh):
    n_dp, n_mp = mesh.shape["dp"], mesh.shape["mp"]
    in_specs = (P("dp", None), P("dp", "mp"), P("dp", "mp"), P("dp", None, "mp"), P("mp", None))
    out_specs = (P("dp", "mp"), P("dp", None, "mp"), P("dp", "mp"), P("mp", None))
    return jax.shard_map(
        functools.partial(local, n_dp, n_mp),
        mesh=mesh, in_specs=in_specs, out_specs=out_specs, check_vma=False,
    )
```

```python
import functools

import jax
import jax.numpy as jnp
from jax import lax
from jax.experimental import pallas as pl
from jax.experimental.pallas import tpu as pltpu
from jax.sharding import PartitionSpec as P

HIGHEST = lax.Precision.HIGHEST
MESH = pl.DeviceIdType.MESH
F32 = jnp.float32
BF16 = jnp.bfloat16
CORES = 2
PANEL = 16
PIECES = 2


def split(x):
    high = x.astype(BF16)
    return high, (x - high.astype(F32)).astype(BF16)


def dot(a, b, da=1, db=0, precision=None):
    return lax.dot_general(
        a, b, (((da,), (db,)), ((), ())), precision=precision, preferred_element_type=F32
    )


def halves(x):
    r = x.shape[1] // 2
    return x[:, :r] + x[:, r:]


def flip(v, r):
    out, bit = v, 1
    while bit <= r:
        if r & bit:
            out = out + bit - 2 * bit * lax.rem(v // bit, 2)
        bit *= 2
    return out


def inverse_factor(gram, work):
    r = gram.shape[0]
    work[...] = gram
    prow = lax.broadcasted_iota(jnp.int32, (PANEL, r), 0)
    lane = lax.broadcasted_iota(jnp.int32, (PANEL, r), 1)
    rows = lax.broadcasted_iota(jnp.int32, (r, r), 0)
    cols = lax.broadcasted_iota(jnp.int32, (r, r), 1)
    for start in range(0, r, PANEL):
        panel = work[start : start + PANEL, :]
        spread = [
            jnp.broadcast_to(panel[:, start + k : start + k + 1], (PANEL, r)) for k in range(PANEL)
        ]
        for t in range(PANEL):
            scale = lax.rsqrt(spread[t][t : t + 1, :])
            below = jnp.where(prow > t, spread[t] * scale, 0.0)
            for k in range(t + 1, PANEL):
                spread[k] = spread[k] - below * (spread[k][t : t + 1, :] * scale)
            panel = jnp.where(lane == start + t, jnp.where(prow == t, 1.0, 0.0), panel)
            row = panel[t : t + 1, :] * scale
            panel = jnp.where(prow == t, row, panel - below * row)
        work[start : start + PANEL, :] = panel
        rest = start + PANEL
        for low, high in ((rest, rest + PANEL), (rest + PANEL, r)):
            if low < min(high, r):
                change = dot(panel[:, low:high], panel, 0, 0, HIGHEST)
                at = cols[low:high]
                old = jnp.where((at >= start) & (at < rest), 0.0, work[low:high, :])
                work[low:high, :] = old - change
    return jnp.where(cols <= rows, work[...], 0.0)


def compress(
    n_dp, n_mp, e_hbm, a_hbm, h_hbm, w_hbm, q_hbm, qn_ref, x_ref, g_ref, e, h,
    a, hall, w, q, q2, p, p2, pt2, tacc, aug, acc, zin, zfin, csend, crecv, xsend, xrecv,
    t, tcrecv, txsend, txrecv, part, zrecv, gsend, grecv,
    l_s, c_s, c_r, x_s, x_r, z_s, z_r, gz_s, gz_r, gx_s, gx_r, gc_s, gc_r,
    tc_s, tc_r, tx_s, tx_r, qx_s, qx_r, qc_s, qc_r, h_s, h_r, w_s, w_r, pz_s, pz_r, gg_s, gg_r,
):
    chips = n_dp // CORES
    me, mp = lax.axis_index("dp"), lax.axis_index("mp")
    chip, core = me // CORES, lax.rem(me, CORES)
    other = 1 - core
    partner = (chip * CORES + other, mp)
    d, rank = p.shape
    ff = t.shape[0]
    tok = a.shape[0]
    pr, tr, tq = d // n_dp, ff // n_dp, tok // n_mp
    wide = CORES * pr
    zr = pr // n_mp if pr % (8 * n_mp) == 0 else pr
    n_sub = chips // n_mp
    goal = chip // n_sub

    def chip_at(r):
        return flip(chip, r)

    def same_core(r):
        return (chip_at(r) * CORES + core, mp)

    def along(r):
        return (me, flip(mp, r))

    def rows(i, n, unit=8):
        return pl.ds(pl.multiple_of(i * n, unit), n)

    def send(src, dst, s, r, to):
        return pltpu.make_async_remote_copy(
            src_ref=src, dst_ref=dst, send_sem=s, recv_sem=r, device_id=to, device_id_type=MESH
        )

    barrier = pltpu.get_barrier_semaphore()
    pl.semaphore_signal(barrier, inc=1, device_id=partner, device_id_type=MESH)
    for r in range(1, chips):
        pl.semaphore_signal(barrier, inc=1, device_id=same_core(r), device_id_type=MESH)
    for r in range(1, n_mp):
        pl.semaphore_signal(barrier, inc=1, device_id=along(r), device_id_type=MESH)
    for s in range(n_sub):
        for q_at in range(n_mp):
            source = mp * n_sub + s

            @pl.when(jnp.logical_or(source != chip, q_at != mp))
            def _():
                pl.semaphore_signal(
                    barrier, inc=1, device_id=(source * CORES + core, q_at), device_id_type=MESH
                )

    loads = []

    def load(src, dst):
        copy = pltpu.make_async_copy(src, dst, l_s.at[len(loads)])
        copy.start()
        loads.append(copy)
        return copy

    h_load = load(h_hbm, h)
    q_load = load(q_hbm, q)
    a_load = load(a_hbm, a)
    order = [chip_at(r) * CORES + other for r in range(1, chips)] + [partner[0]]
    order += [chip_at(r) * CORES + core for r in range(1, chips)] + [me]
    e_loads = [load(e_hbm.at[rows(b, pr, 16), :], e.at[rows(b, pr, 16), :]) for b in order]
    w_load = load(w_hbm, w.at[rows(core, pr, 16), :])

    pl.semaphore_wait(barrier, 1 + (chips - 1) + (n_mp - 1) + chips - jnp.where(goal == mp, 1, 0))

    tp = tok // PIECES
    h_copies = {}

    def send_hidden(r, k):
        at = pl.ds(k * tp, tp)
        i = r * PIECES + k
        copy = send(h_hbm.at[at, :], hall.at[r - 1, at, :], h_s.at[i], h_r.at[i], same_core(r))
        copy.start()
        h_copies[r, k] = copy

    near = [r for r in range(1, chips) if r & (r - 1) == 0]
    far = [r for r in range(1, chips) if r & (r - 1) != 0]
    for r in near:
        send_hidden(r, 0)
    w_copy = send(w_hbm, w.at[rows(core, pr, 16), :], w_s.at[0], w_r.at[0], partner)
    w_copy.start()

    h_load.wait()
    q_load.wait()
    q_high, q_low = split(q[...])
    q2[:, :rank] = q_high
    q2[:, rank:] = q_low
    hq = halves(dot(h[...], q2[...]))
    hq2 = jnp.concatenate(split(hq), axis=1)
    a_load.wait()
    p[...] = halves(dot(a[...], hq2, 0, 0))

    def project(i):
        e_loads[i].wait()
        at = rows(order[i], pr, 16)
        return halves(dot(e[at, :], q2[...])) + p[at, :]

    core_copies = []
    for i in range(chips):
        csend[i] = project(i)
        copy = send(csend.at[i], crecv.at[i], c_s.at[i], c_r.at[i], partner)
        copy.start()
        core_copies.append(copy)
    x_copies = []
    for i in range(chips):
        value = project(chips + i)
        core_copies[i].wait_recv()
        value = value + crecv[i]
        if i < chips - 1:
            xsend[i] = value
            copy = send(xsend.at[i], xrecv.at[i], x_s.at[i], x_r.at[i], same_core(i + 1))
            copy.start()
            x_copies.append(copy)
        else:
            acc[...] = value

    z_parts = {}

    def partial_input(r):
        part[r] = dot(hall[r - 1] if r else h[...], w[...], 1, 1)

    def send_partial(r):
        for s in range(1, n_mp):
            i = r * n_mp + s
            copy = send(
                part.at[r, rows(flip(mp, s), tq), :], zrecv.at[r, s - 1],
                pz_s.at[i], pz_r.at[i], along(s),
            )
            copy.start()
            z_parts[r, s] = copy

    w_load.wait()
    w_copy.wait_recv()
    partial_input(0)
    send_partial(0)

    value = acc[...]
    for i, copy in enumerate(x_copies):
        copy.wait_recv()
        value = value + xrecv[i]
    acc[...] = value
    for r in near:
        for k in range(1, PIECES):
            send_hidden(r, k)

    def segment(i):
        return rows(i, zr) if zr < pr else pl.ds(0, pr)

    z_copies = []
    for r in range(1, n_mp):
        copy = send(
            acc.at[segment(flip(mp, r)), :], zin.at[r - 1], z_s.at[r - 1], z_r.at[r - 1], along(r)
        )
        copy.start()
        z_copies.append(copy)
    value = acc[segment(mp), :]
    for r in far:
        for k in range(PIECES):
            send_hidden(r, k)
    for i, copy in enumerate(z_copies):
        copy.wait_recv()
        value = value + zin[i]
    if zr < pr:
        zfin[...] = value
        here = pl.ds(pl.multiple_of(me * pr + mp * zr, 8), zr)
        p[here, :] = value
        gz = []
        for r in range(1, n_mp):
            copy = send(zfin, p.at[here, :], gz_s.at[r - 1], gz_r.at[r - 1], along(r))
            copy.start()
            gz.append(copy)
        for copy in gz:
            copy.wait_recv()
        z_copies += gz
    else:
        p[rows(me, pr), :] = value

    class Gather:
        def __init__(self, ref, n, x_s, x_r, c_s, c_r):
            self.ref, self.n = ref, n
            self.x_s, self.x_r, self.c_s, self.c_r = x_s, x_r, c_s, c_r
            own = rows(me, n)
            self.across, self.down = {}, {}
            for r in range(1, chips):
                copy = send(ref.at[own, :], ref.at[own, :], x_s.at[r], x_r.at[r], same_core(r))
                copy.start()
                self.across[r] = copy
            self.forward(0)

        def forward(self, r):
            if r:
                self.across[r].wait_recv()
            at = rows(chip_at(r) * CORES + core, self.n)
            copy = send(self.ref.at[at, :], self.ref.at[at, :], self.c_s.at[r], self.c_r.at[r], partner)
            copy.start()
            self.down[r] = copy

        def finish(self):
            for copy in list(self.across.values()) + list(self.down.values()):
                copy.wait_send()

    for copy in core_copies + x_copies + z_copies:
        copy.wait_send()
    gather = Gather(p, pr, gx_s, gx_r, gc_s, gc_r)

    for r in near:
        for k in range(PIECES):
            h_copies[r, k].wait_recv()
        partial_input(r)
        send_partial(r)

    width = 256

    def accumulate(r, gram):
        gather.down[r].wait_recv()
        at = pl.ds(pl.multiple_of(chip_at(r) * wide, 16), wide)
        block = p[at, :]
        high, low = split(block)
        p2[at, :rank] = high
        p2[at, rank:] = low
        turned = block.T
        high, low = split(turned)
        pt2[:rank, :] = high
        pt2[rank:, :] = low
        last = r == chips - 1
        if last:
            ap = halves(dot(a[...], p2[...])).T
            ap2 = jnp.concatenate(split(ap), axis=0)

        def term(n, carry):
            cols = pl.ds(pl.multiple_of(n * width, width), width)
            both = dot(pt2[...], e[at, cols])
            total = both[:rank] + both[rank:]
            if r:
                total = total + tacc[:, cols]
            if last:
                both = dot(ap2, h[:, cols])
                t[cols, :] = (total + (both[:rank] + both[rank:])).T
            else:
                tacc[:, cols] = total
            return carry

        lax.fori_loop(0, ff // width, term, 0)
        return lambda: gram + dot(turned, block, 1, 0, HIGHEST)

    gram = accumulate(0, 0.0)()
    for r in near:
        gather.forward(r)
    for r in range(1, chips - 1):
        if r in far:
            gather.forward(r)
        gram = accumulate(r, gram)()
    gather.forward(chips - 1)
    add_gram = accumulate(chips - 1, gram)

    t_copies = []
    for i in range(chips):
        block = chip_at((i + 1) % chips) * CORES + other
        copy = send(t.at[rows(block, tr), :], tcrecv.at[i], tc_s.at[i], tc_r.at[i], partner)
        copy.start()
        t_copies.append(copy)
    gram = add_gram()
    tx_copies = []
    for i in range(chips):
        t_copies[i].wait_recv()
        value = t[rows(chip_at((i + 1) % chips) * CORES + core, tr), :] + tcrecv[i]
        txsend[i] = value
        if i < chips - 1:
            copy = send(txsend.at[i], txrecv.at[i], tx_s.at[i], tx_r.at[i], same_core(i + 1))
            copy.start()
            tx_copies.append(copy)
    for r in far:
        for k in range(PIECES):
            h_copies[r, k].wait_recv()
        partial_input(r)
        send_partial(r)
    inverse = inverse_factor(gram, aug)
    value = txsend[chips - 1]
    for i, copy in enumerate(tx_copies):
        copy.wait_recv()
        value = value + txrecv[i]
    qn_ref[rows(me, tr), :] = dot(value, inverse, 1, 1, HIGHEST) / n_dp
    gather.finish()
    gather = Gather(qn_ref, tr, qx_s, qx_r, qc_s, qc_r)

    g_copies = []
    for r in range(chips):
        value = part[r, rows(mp, tq), :]
        for s in range(1, n_mp):
            z_parts[r, s].wait_recv()
            value = value + zrecv[r, s - 1]
        gsend[r] = value.astype(BF16)
        place = grecv.at[lax.rem(chip, n_sub), rows(mp, tq, 16), :]
        slot = lax.rem(chip, n_sub) * n_mp + mp
        to = (chip_at(r) * CORES + core, goal)
        copy = send(gsend.at[r], place, gg_s.at[r], gg_r.at[slot], to)
        if r:
            copy.start()
        else:

            @pl.when(goal != mp)
            def _():
                copy.start()

            @pl.when(goal == mp)
            def _():
                place[...] = gsend[0]

        g_copies.append(copy)

    high, low = split(dot(p[...], inverse, 1, 1, HIGHEST))
    x_ref[:, :rank] = high
    x_ref[:, rank : 2 * rank] = low
    x_ref[:, 2 * rank : 3 * rank] = high
    x_ref[:, 3 * rank :] = a[...].T

    for r in range(1, chips):
        gather.forward(r)
    for s in range(n_sub):
        for q_at in range(n_mp):
            at = pl.ds(q_at * tq, tq)
            arrival = send(
                gsend.at[0], grecv.at[s, at, :], gg_s.at[0], gg_r.at[s * n_mp + q_at], partner
            )

            @pl.when(jnp.logical_or(mp * n_sub + s != chip, q_at != mp))
            def _():
                arrival.wait_recv()

        g_ref[:, s * wide : (s + 1) * wide] = grecv[s]
    for copy in gather.down.values():
        copy.wait_recv()
    gather.finish()
    for copy in t_copies + tx_copies + list(h_copies.values()) + list(z_parts.values()) + [w_copy]:
        copy.wait_send()
    for r in range(1, chips):
        g_copies[r].wait_send()

    @pl.when(goal != mp)
    def _():
        g_copies[0].wait_send()


def residual(
    n_dp, width, e_ref, h_ref, qn_ref, x_ref, g_ref, out_hbm, up_hbm, q_hbm, g_hbm,
    y, out, up, o_s, u_s, k_s,
):
    d, ff = e_ref.shape
    rank = qn_ref.shape[1]
    share = up_hbm.shape[0]
    parts = d // out.shape[1]
    block = out.shape[1]
    copies = []

    def store(src, dst, sem):
        copy = pltpu.make_async_copy(src, dst, sem)
        copy.start()
        copies.append(copy)

    store(qn_ref, q_hbm, k_s.at[0])
    store(g_ref, g_hbm, k_s.at[1])
    own = pl.ds(pl.multiple_of(lax.axis_index("dp") * share, 16), share)
    for j in range(ff // width):
        cols = slice(j * width, (j + 1) * width)
        high, low = split(-qn_ref[cols, :].T)
        y[j, :rank] = high
        y[j, rank : 2 * rank] = high
        y[j, 2 * rank : 3 * rank] = low
        y[j, 3 * rank :] = h_ref[:, cols]
        up[j] = -dot(x_ref[own, : 3 * rank], y[j, : 3 * rank])
        store(up.at[j], up_hbm.at[:, cols], u_s.at[j])
        for i in range(parts):
            at = slice(i * block, (i + 1) * block)
            n = j * parts + i
            out[n] = (e_ref[at, cols].astype(F32) + dot(x_ref[at, :], y[j])).astype(BF16)
            store(out.at[n], out_hbm.at[at, cols], o_s.at[n])
    for copy in copies:
        copy.wait()


def local(n_dp, n_mp, activations, grad_hidden, up_weight, error_feedback, query_previous):
    error = error_feedback[0]
    d, ff = error.shape
    tok, rank = activations.shape[0], query_previous.shape[1]
    chips = n_dp // CORES
    pr, tr, tq = d // n_dp, ff // n_dp, tok // n_mp
    wide = CORES * pr
    zr = pr // n_mp if pr % (8 * n_mp) == 0 else pr
    n_sub = chips // n_mp
    vmem = pl.BlockSpec(memory_space=pltpu.VMEM)
    hbm = pl.BlockSpec(memory_space=pl.ANY)
    dma = pltpu.SemaphoreType.DMA
    pairs = lambda n: [dma((n,)), dma((n,))]
    arguments = [
        pltpu.with_memory_space_constraint(x, pltpu.HBM)
        for x in (error, activations, grad_hidden, up_weight, query_previous)
    ]
    query_next, factors, grad_input, error_held, hidden_held = pl.pallas_call(
        functools.partial(compress, n_dp, n_mp),
        out_shape=(
            pltpu.VMEM((ff, rank), F32),
            pltpu.VMEM((d, 3 * rank + tok), BF16),
            pltpu.VMEM((tok, d // n_mp), BF16),
            pltpu.VMEM((d, ff), BF16),
            pltpu.VMEM((tok, ff), BF16),
        ),
        in_specs=[hbm] * 5,
        out_specs=(vmem,) * 5,
        scratch_shapes=[
            pltpu.VMEM((tok, d), BF16),
            pltpu.VMEM((chips - 1, tok, ff), BF16),
            pltpu.VMEM((wide, ff), BF16),
            pltpu.VMEM((ff, rank), F32),
            pltpu.VMEM((ff, 2 * rank), BF16),
            pltpu.VMEM((d, rank), F32),
            pltpu.VMEM((d, 2 * rank), BF16),
            pltpu.VMEM((2 * rank, wide), BF16),
            pltpu.VMEM((rank, ff), F32),
            pltpu.VMEM((rank, rank), F32),
            pltpu.VMEM((pr, rank), F32),
            pltpu.VMEM((n_mp, zr, rank), F32),
            pltpu.VMEM((zr, rank), F32),
            pltpu.VMEM((chips, pr, rank), F32),
            pltpu.VMEM((chips, pr, rank), F32),
            pltpu.VMEM((chips, pr, rank), F32),
            pltpu.VMEM((chips, pr, rank), F32),
            pltpu.VMEM((ff, rank), F32),
            pltpu.VMEM((chips, tr, rank), F32),
            pltpu.VMEM((chips, tr, rank), F32),
            pltpu.VMEM((chips, tr, rank), F32),
            pltpu.VMEM((chips, tok, wide), F32),
            pltpu.VMEM((chips, n_mp - 1, tq, wide), F32),
            pltpu.VMEM((chips, tq, wide), BF16),
            pltpu.VMEM((n_sub, tok, wide), BF16),
            dma((n_dp + 4,)),
        ]
        + pairs(chips) + pairs(chips) + pairs(n_mp) + pairs(n_mp) + pairs(chips) + pairs(chips)
        + pairs(chips) + pairs(chips) + pairs(chips) + pairs(chips)
        + pairs(PIECES * chips) + pairs(1) + pairs(chips * n_mp) + pairs(chips),
        compiler_params=pltpu.CompilerParams(
            collective_id=0, has_side_effects=True, vmem_limit_bytes=34 << 20
        ),
        cost_estimate=pl.CostEstimate(flops=64 * d * ff * rank, bytes_accessed=48 * d * ff, transcendentals=0),
        name="compress",
    )(*arguments)

    width, parts = min(512, ff), 4
    error_next, update, query_out, grad_out = pl.pallas_call(
        functools.partial(residual, n_dp, width),
        out_shape=(
            jax.ShapeDtypeStruct((d, ff), BF16),
            jax.ShapeDtypeStruct((pr, ff), F32),
            jax.ShapeDtypeStruct((ff, rank), F32),
            jax.ShapeDtypeStruct((tok, d // n_mp), BF16),
        ),
        in_specs=[vmem] * 5,
        out_specs=(hbm,) * 4,
        scratch_shapes=[
            pltpu.VMEM((ff // width, 3 * rank + tok, width), BF16),
            pltpu.VMEM((ff // width * parts, d // parts, width), BF16),
            pltpu.VMEM((ff // width, pr, width), F32),
            dma((ff // width * parts,)),
            dma((ff // width,)),
            dma((2,)),
        ],
        compiler_params=pltpu.CompilerParams(vmem_limit_bytes=26 << 20),
        cost_estimate=pl.CostEstimate(flops=8 * d * ff * rank, bytes_accessed=4 * d * ff, transcendentals=0),
        name="residual",
    )(error_held, hidden_held, query_next, factors, grad_input)
    return grad_out, error_next[None], update, query_out


def solution(mesh):
    n_dp, n_mp = mesh.shape["dp"], mesh.shape["mp"]
    in_specs = (P("dp", None), P("dp", "mp"), P("dp", "mp"), P("dp", None, "mp"), P("mp", None))
    out_specs = (P("dp", "mp"), P("dp", None, "mp"), P("dp", "mp"), P("mp", None))
    return jax.shard_map(
        functools.partial(local, n_dp, n_mp),
        mesh=mesh, in_specs=in_specs, out_specs=out_specs, check_vma=False,
    )
```

```python
import functools

import jax
import jax.numpy as jnp
from jax import lax
from jax.experimental import pallas as pl
from jax.experimental.pallas import tpu as pltpu
from jax.sharding import PartitionSpec as P

HIGHEST = lax.Precision.HIGHEST
MESH = pl.DeviceIdType.MESH
F32 = jnp.float32
BF16 = jnp.bfloat16
CORES = 2
PANEL = 16
PIECES = 2
CHUNKS = 2


def split(x):
    high = x.astype(BF16)
    return high, (x - high.astype(F32)).astype(BF16)


def dot(a, b, da=1, db=0, precision=None):
    return lax.dot_general(
        a, b, (((da,), (db,)), ((), ())), precision=precision, preferred_element_type=F32
    )


def halves(x):
    r = x.shape[1] // 2
    return x[:, :r] + x[:, r:]


def flip(v, r):
    out, bit = v, 1
    while bit <= r:
        if r & bit:
            out = out + bit - 2 * bit * lax.rem(v // bit, 2)
        bit *= 2
    return out


def bits_of(r):
    return [1 << b for b in range(r.bit_length()) if r >> b & 1]


def inverse_factor(gram, work):
    r = gram.shape[0]
    work[...] = gram
    prow = lax.broadcasted_iota(jnp.int32, (PANEL, r), 0)
    lane = lax.broadcasted_iota(jnp.int32, (PANEL, r), 1)
    rows = lax.broadcasted_iota(jnp.int32, (r, r), 0)
    cols = lax.broadcasted_iota(jnp.int32, (r, r), 1)
    for start in range(0, r, PANEL):
        panel = work[start : start + PANEL, :]
        spread = [
            jnp.broadcast_to(panel[:, start + k : start + k + 1], (PANEL, r)) for k in range(PANEL)
        ]
        for t in range(PANEL):
            scale = lax.rsqrt(spread[t][t : t + 1, :])
            below = jnp.where(prow > t, spread[t] * scale, 0.0)
            for k in range(t + 1, PANEL):
                spread[k] = spread[k] - below * (spread[k][t : t + 1, :] * scale)
            panel = jnp.where(lane == start + t, jnp.where(prow == t, 1.0, 0.0), panel)
            row = panel[t : t + 1, :] * scale
            panel = jnp.where(prow == t, row, panel - below * row)
        work[start : start + PANEL, :] = panel
        rest = start + PANEL
        for low, high in ((rest, rest + PANEL), (rest + PANEL, r)):
            if low < min(high, r):
                change = dot(panel[:, low:high], panel, 0, 0, HIGHEST)
                at = cols[low:high]
                old = jnp.where((at >= start) & (at < rest), 0.0, work[low:high, :])
                work[low:high, :] = old - change
    return jnp.where(cols <= rows, work[...], 0.0)


def compress(
    n_dp, n_mp, e_hbm, a_hbm, h_hbm, w_hbm, q_hbm, qn_ref, x_ref, g_ref, e, h,
    a, hall, w, q, q2, p, p2, pt2, tacc, aug, acc, zin, zfin, csend, crecv, xsend, xrecv,
    t, tcrecv, txsend, txrecv, part, zrecv, gsend, grecv,
    l_s, c_s, c_r, x_s, x_r, z_s, z_r, gz_s, gz_r, gx_s, gx_r, gc_s, gc_r,
    tc_s, tc_r, tx_s, tx_r, qx_s, qx_r, qc_s, qc_r, h_s, h_r, w_s, w_r, pz_s, pz_r, gg_s, gg_r,
):
    chips = n_dp // CORES
    me, mp = lax.axis_index("dp"), lax.axis_index("mp")
    chip, core = me // CORES, lax.rem(me, CORES)
    other = 1 - core
    partner = (chip * CORES + other, mp)
    d, rank = p.shape
    ff = t.shape[0]
    tok = a.shape[0]
    pr, tr, tq = d // n_dp, ff // n_dp, tok // n_mp
    wide = CORES * pr
    pc, tc = pr // CHUNKS, tr // CHUNKS
    zr = pc // n_mp if pc % (8 * n_mp) == 0 else pc
    n_sub = chips // n_mp
    goal = chip // n_sub

    def chip_at(r):
        return flip(chip, r)

    def same_core(r):
        return (chip_at(r) * CORES + core, mp)

    def along(r):
        return (me, flip(mp, r))

    def rows(i, n, unit=8):
        return pl.ds(pl.multiple_of(i * n, unit), n)

    def send(src, dst, s, r, to):
        return pltpu.make_async_remote_copy(
            src_ref=src, dst_ref=dst, send_sem=s, recv_sem=r, device_id=to, device_id_type=MESH
        )

    barrier = pltpu.get_barrier_semaphore()
    pl.semaphore_signal(barrier, inc=1, device_id=partner, device_id_type=MESH)
    for r in range(1, chips):
        pl.semaphore_signal(barrier, inc=1, device_id=same_core(r), device_id_type=MESH)
    for r in range(1, n_mp):
        pl.semaphore_signal(barrier, inc=1, device_id=along(r), device_id_type=MESH)
    for s in range(n_sub):
        for q_at in range(n_mp):
            source = mp * n_sub + s

            @pl.when(jnp.logical_or(source != chip, q_at != mp))
            def _():
                pl.semaphore_signal(
                    barrier, inc=1, device_id=(source * CORES + core, q_at), device_id_type=MESH
                )

    loads = []

    def load(src, dst):
        copy = pltpu.make_async_copy(src, dst, l_s.at[len(loads)])
        copy.start()
        loads.append(copy)
        return copy

    h_load = load(h_hbm, h)
    q_load = load(q_hbm, q)
    a_load = load(a_hbm, a)
    order = [chip_at(r) * CORES + other for r in range(1, chips)] + [partner[0]]
    order += [chip_at(r) * CORES + core for r in range(1, chips)] + [me]
    e_loads = [load(e_hbm.at[rows(b, pr, 16), :], e.at[rows(b, pr, 16), :]) for b in order]
    w_load = load(w_hbm, w.at[rows(core, pr, 16), :])

    pl.semaphore_wait(barrier, 1 + (chips - 1) + (n_mp - 1) + chips - jnp.where(goal == mp, 1, 0))

    tp = tok // PIECES
    h_copies = {}
    near = [r for r in range(1, chips) if len(bits_of(r)) == 1]
    pair = [r for r in range(1, chips) if len(bits_of(r)) == 2]
    many = [r for r in range(1, chips) if len(bits_of(r)) > 2]

    def send_hidden(r, k):
        at = pl.ds(k * tp, tp)
        i = r * PIECES + k
        copy = send(h_hbm.at[at, :], hall.at[r - 1, at, :], h_s.at[i], h_r.at[i], same_core(r))
        copy.start()
        h_copies[r, k] = copy

    def relay_hidden(r, k):
        via, to = bits_of(r) if k % 2 == 0 else bits_of(r)[::-1]
        at = pl.ds(k * tp, tp)
        i = r * PIECES + k
        copy = send(
            hall.at[via - 1, at, :], hall.at[r - 1, at, :], h_s.at[i], h_r.at[i], same_core(to)
        )
        copy.start()
        h_copies[r, k] = copy

    for r in near:
        send_hidden(r, 0)
    w_copy = send(w_hbm, w.at[rows(core, pr, 16), :], w_s.at[0], w_r.at[0], partner)
    w_copy.start()

    h_load.wait()
    q_load.wait()
    q_high, q_low = split(q[...])
    q2[:, :rank] = q_high
    q2[:, rank:] = q_low
    hq = halves(dot(h[...], q2[...]))
    hq2 = jnp.concatenate(split(hq), axis=1)
    a_load.wait()
    p[...] = halves(dot(a[...], hq2, 0, 0))

    def project(i):
        e_loads[i].wait()
        at = rows(order[i], pr, 16)
        return halves(dot(e[at, :], q2[...])) + p[at, :]

    core_copies = []
    for i in range(chips):
        csend[i] = project(i)
        copy = send(csend.at[i], crecv.at[i], c_s.at[i], c_r.at[i], partner)
        copy.start()
        core_copies.append(copy)
    x_copies = {}

    def send_chunk(i, k):
        at = pl.ds(k * pc, pc)
        n = i * CHUNKS + k
        copy = send(xsend.at[i, at, :], xrecv.at[i, at, :], x_s.at[n], x_r.at[n], same_core(i + 1))
        copy.start()
        x_copies[i, k] = copy

    for i in range(chips):
        value = project(chips + i)
        core_copies[i].wait_recv()
        xsend[i] = value + crecv[i]
        if i < chips - 1:
            send_chunk(i, 0)
    for k in range(1, CHUNKS):
        for i in range(chips - 1):
            send_chunk(i, k)

    z_parts = {}

    def partial_input(r):
        part[r] = dot(hall[r - 1] if r else h[...], w[...], 1, 1)

    def send_partial(r):
        for s in range(1, n_mp):
            i = r * n_mp + s
            copy = send(
                part.at[r, rows(flip(mp, s), tq), :], zrecv.at[r, s - 1],
                pz_s.at[i], pz_r.at[i], along(s),
            )
            copy.start()
            z_parts[r, s] = copy

    w_load.wait()
    w_copy.wait_recv()
    partial_input(0)
    send_partial(0)

    def segment(k, i):
        return rows(i, zr) if zr < pc else pl.ds(0, pc)

    z_copies, gz = {}, {}
    for k in range(CHUNKS):
        at = pl.ds(k * pc, pc)
        value = xsend[chips - 1, at, :]
        for i in range(chips - 1):
            x_copies[i, k].wait_recv()
            value = value + xrecv[i, at, :]
        acc[k] = value
        for r in range(1, n_mp):
            n = k * n_mp + r
            copy = send(
                acc.at[k, segment(k, flip(mp, r)), :], zin.at[k, r], z_s.at[n], z_r.at[n], along(r)
            )
            copy.start()
            z_copies[r, k] = copy
    for r in near:
        for k in range(1, PIECES):
            send_hidden(r, k)
    for k in range(CHUNKS):
        value = acc[k, segment(k, mp), :]
        for r in range(1, n_mp):
            z_copies[r, k].wait_recv()
            value = value + zin[k, r]
        if zr < pc:
            zfin[k] = value
            here = pl.ds(pl.multiple_of(me * pr + k * pc + mp * zr, 8), zr)
            p[here, :] = value
            for r in range(1, n_mp):
                n = k * n_mp + r
                copy = send(zfin.at[k], p.at[here, :], gz_s.at[n], gz_r.at[n], along(r))
                copy.start()
                gz[r, k] = copy
        else:
            p[pl.ds(pl.multiple_of(me * pr + k * pc, 8), pc), :] = value

    class Gather:
        def __init__(self, ref, n, x_s, x_r, c_s, c_r):
            self.ref, self.n = ref, n
            self.x_s, self.x_r, self.c_s, self.c_r = x_s, x_r, c_s, c_r
            self.across, self.down = {}, {}

        def at(self, r, k):
            part = self.n // CHUNKS
            base = (chip_at(r) * CORES + core) * self.n + k * part
            return self.ref.at[pl.ds(pl.multiple_of(base, 8), part), :]

        def out(self, origin, r, k, to):
            block, n = self.at(origin, k), r * CHUNKS + k
            copy = send(block, block, self.x_s.at[n], self.x_r.at[n], same_core(to))
            copy.start()
            self.across[r, k] = copy

        def begin(self, k):
            for r in near + many:
                self.out(0, r, k, r)
            self.hand(0, k)

        def hand(self, r, k):
            block, n = self.at(r, k), r * CHUNKS + k
            copy = send(block, block, self.c_s.at[n], self.c_r.at[n], partner)
            copy.start()
            self.down[r, k] = copy

        def relay(self, r, k):
            self.across[r, k].wait_recv()
            for f in pair:
                via, to = bits_of(f) if k % 2 == 0 else bits_of(f)[::-1]
                if r == via:
                    self.out(r, f, k, to)
            self.hand(r, k)

        def wait(self, r):
            for k in range(CHUNKS):
                self.down[r, k].wait_recv()

        def finish(self):
            for copy in list(self.across.values()) + list(self.down.values()):
                copy.wait_send()

    gather = Gather(p, pr, gx_s, gx_r, gc_s, gc_r)
    for k in range(CHUNKS):
        if zr < pc:
            for r in range(1, n_mp):
                gz[r, k].wait_recv()
        gather.begin(k)

    width = 256

    def accumulate(r, gram):
        gather.wait(r)
        at = pl.ds(pl.multiple_of(chip_at(r) * wide, 16), wide)
        block = p[at, :]
        high, low = split(block)
        p2[at, :rank] = high
        p2[at, rank:] = low
        turned = block.T
        high, low = split(turned)
        pt2[:rank, :] = high
        pt2[rank:, :] = low
        last = r == chips - 1
        if last:
            ap = halves(dot(a[...], p2[...])).T
            ap2 = jnp.concatenate(split(ap), axis=0)

        def term(n, carry):
            cols = pl.ds(pl.multiple_of(n * width, width), width)
            both = dot(pt2[...], e[at, cols])
            total = both[:rank] + both[rank:]
            if r:
                total = total + tacc[:, cols]
            if last:
                both = dot(ap2, h[:, cols])
                t[cols, :] = (total + (both[:rank] + both[rank:])).T
            else:
                tacc[:, cols] = total
            return carry

        lax.fori_loop(0, ff // width, term, 0, unroll=True)
        return lambda: gram + dot(turned, block, 1, 0, HIGHEST)

    gram = accumulate(0, 0.0)()
    for r in near:
        gather.relay(r, 0)
    for r in near:
        for k in range(PIECES):
            h_copies[r, k].wait_recv()
        partial_input(r)
        send_partial(r)
    for k in range(1, CHUNKS):
        for r in near:
            gather.relay(r, k)
    for r in near:
        gram = accumulate(r, gram)()
    for r in many + pair[:-1]:
        for k in range(CHUNKS):
            gather.relay(r, k)
        gram = accumulate(r, gram)()
    for k in range(CHUNKS):
        gather.relay(pair[-1], k)
    for k in range(PIECES):
        for r in pair:
            relay_hidden(r, k)
        for r in many:
            send_hidden(r, k)
    add_gram = accumulate(pair[-1], gram)

    t_copies = []
    for i in range(chips):
        block = chip_at((i + 1) % chips) * CORES + other
        copy = send(t.at[rows(block, tr), :], tcrecv.at[i], tc_s.at[i], tc_r.at[i], partner)
        copy.start()
        t_copies.append(copy)
    gram = add_gram()
    tx_copies = {}

    def send_term(i, k):
        at = pl.ds(k * tc, tc)
        n = i * CHUNKS + k
        copy = send(txsend.at[i, at, :], txrecv.at[i, at, :], tx_s.at[n], tx_r.at[n], same_core(i + 1))
        copy.start()
        tx_copies[i, k] = copy

    for i in range(chips):
        t_copies[i].wait_recv()
        txsend[i] = t[rows(chip_at((i + 1) % chips) * CORES + core, tr), :] + tcrecv[i]
        if i < chips - 1:
            send_term(i, 0)
    for k in range(1, CHUNKS):
        for i in range(chips - 1):
            send_term(i, k)
    inverse = inverse_factor(gram, aug)
    gather.finish()
    gather = Gather(qn_ref, tr, qx_s, qx_r, qc_s, qc_r)
    for k in range(CHUNKS):
        at = pl.ds(k * tc, tc)
        value = txsend[chips - 1, at, :]
        for i in range(chips - 1):
            tx_copies[i, k].wait_recv()
            value = value + txrecv[i, at, :]
        own = pl.ds(pl.multiple_of(me * tr + k * tc, 8), tc)
        qn_ref[own, :] = dot(value, inverse, 1, 1, HIGHEST) / n_dp
        gather.begin(k)
    for r in pair + many:
        for k in range(PIECES):
            h_copies[r, k].wait_recv()
        partial_input(r)
        send_partial(r)
    for r in near:
        gather.relay(r, 0)
    high, low = split(dot(p[...], inverse, 1, 1, HIGHEST))
    x_ref[:, :rank] = high
    x_ref[:, rank : 2 * rank] = low
    x_ref[:, 2 * rank : 3 * rank] = high
    x_ref[:, 3 * rank :] = a[...].T
    for k in range(1, CHUNKS):
        for r in near:
            gather.relay(r, k)

    g_copies = []
    for r in range(chips):
        value = part[r, rows(mp, tq), :]
        for s in range(1, n_mp):
            z_parts[r, s].wait_recv()
            value = value + zrecv[r, s - 1]
        gsend[r] = value.astype(BF16)
        place = grecv.at[lax.rem(chip, n_sub), rows(mp, tq, 16), :]
        slot = lax.rem(chip, n_sub) * n_mp + mp
        to = (chip_at(r) * CORES + core, goal)
        copy = send(gsend.at[r], place, gg_s.at[r], gg_r.at[slot], to)
        if r:
            copy.start()
        else:

            @pl.when(goal != mp)
            def _():
                copy.start()

            @pl.when(goal == mp)
            def _():
                place[...] = gsend[0]

        g_copies.append(copy)

    for r in pair + many:
        for k in range(CHUNKS):
            gather.relay(r, k)
    for s in range(n_sub):
        for q_at in range(n_mp):
            at = pl.ds(q_at * tq, tq)
            arrival = send(
                gsend.at[0], grecv.at[s, at, :], gg_s.at[0], gg_r.at[s * n_mp + q_at], partner
            )

            @pl.when(jnp.logical_or(mp * n_sub + s != chip, q_at != mp))
            def _():
                arrival.wait_recv()

        g_ref[:, s * wide : (s + 1) * wide] = grecv[s]
    for r in range(chips):
        gather.wait(r)
    gather.finish()
    started = [w_copy] + core_copies + t_copies
    for copies in (x_copies, z_copies, gz, tx_copies, h_copies, z_parts):
        started += list(copies.values())
    for copy in started:
        copy.wait_send()
    for r in range(1, chips):
        g_copies[r].wait_send()

    @pl.when(goal != mp)
    def _():
        g_copies[0].wait_send()


def residual(
    n_dp, width, e_ref, h_ref, qn_ref, x_ref, g_ref, out_hbm, up_hbm, q_hbm, g_hbm,
    y, out, up, o_s, u_s, k_s,
):
    d, ff = e_ref.shape
    rank = qn_ref.shape[1]
    share = up_hbm.shape[0]
    parts = d // out.shape[1]
    block = out.shape[1]
    copies = []

    def store(src, dst, sem):
        copy = pltpu.make_async_copy(src, dst, sem)
        copy.start()
        copies.append(copy)

    store(qn_ref, q_hbm, k_s.at[0])
    store(g_ref, g_hbm, k_s.at[1])
    own = pl.ds(pl.multiple_of(lax.axis_index("dp") * share, 16), share)
    for j in range(ff // width):
        cols = slice(j * width, (j + 1) * width)
        high, low = split(-qn_ref[cols, :].T)
        y[j, :rank] = high
        y[j, rank : 2 * rank] = high
        y[j, 2 * rank : 3 * rank] = low
        y[j, 3 * rank :] = h_ref[:, cols]
        up[j] = -dot(x_ref[own, : 3 * rank], y[j, : 3 * rank])
        store(up.at[j], up_hbm.at[:, cols], u_s.at[j])
        for i in range(parts):
            at = slice(i * block, (i + 1) * block)
            n = j * parts + i
            out[n] = (e_ref[at, cols].astype(F32) + dot(x_ref[at, :], y[j])).astype(BF16)
            store(out.at[n], out_hbm.at[at, cols], o_s.at[n])
    for copy in copies:
        copy.wait()


def local(n_dp, n_mp, activations, grad_hidden, up_weight, error_feedback, query_previous):
    error = error_feedback[0]
    d, ff = error.shape
    tok, rank = activations.shape[0], query_previous.shape[1]
    chips = n_dp // CORES
    pr, tr, tq = d // n_dp, ff // n_dp, tok // n_mp
    wide = CORES * pr
    pc = pr // CHUNKS
    zr = pc // n_mp if pc % (8 * n_mp) == 0 else pc
    n_sub = chips // n_mp
    many = CHUNKS * chips
    vmem = pl.BlockSpec(memory_space=pltpu.VMEM)
    hbm = pl.BlockSpec(memory_space=pl.ANY)
    dma = pltpu.SemaphoreType.DMA
    pairs = lambda n: [dma((n,)), dma((n,))]
    arguments = [
        pltpu.with_memory_space_constraint(x, pltpu.HBM)
        for x in (error, activations, grad_hidden, up_weight, query_previous)
    ]
    query_next, factors, grad_input, error_held, hidden_held = pl.pallas_call(
        functools.partial(compress, n_dp, n_mp),
        out_shape=(
            pltpu.VMEM((ff, rank), F32),
            pltpu.VMEM((d, 3 * rank + tok), BF16),
            pltpu.VMEM((tok, d // n_mp), BF16),
            pltpu.VMEM((d, ff), BF16),
            pltpu.VMEM((tok, ff), BF16),
        ),
        in_specs=[hbm] * 5,
        out_specs=(vmem,) * 5,
        scratch_shapes=[
            pltpu.VMEM((tok, d), BF16),
            pltpu.VMEM((chips - 1, tok, ff), BF16),
            pltpu.VMEM((wide, ff), BF16),
            pltpu.VMEM((ff, rank), F32),
            pltpu.VMEM((ff, 2 * rank), BF16),
            pltpu.VMEM((d, rank), F32),
            pltpu.VMEM((d, 2 * rank), BF16),
            pltpu.VMEM((2 * rank, wide), BF16),
            pltpu.VMEM((rank, ff), F32),
            pltpu.VMEM((rank, rank), F32),
            pltpu.VMEM((CHUNKS, pc, rank), F32),
            pltpu.VMEM((CHUNKS, n_mp, zr, rank), F32),
            pltpu.VMEM((CHUNKS, zr, rank), F32),
            pltpu.VMEM((chips, pr, rank), F32),
            pltpu.VMEM((chips, pr, rank), F32),
            pltpu.VMEM((chips, pr, rank), F32),
            pltpu.VMEM((chips, pr, rank), F32),
            pltpu.VMEM((ff, rank), F32),
            pltpu.VMEM((chips, tr, rank), F32),
            pltpu.VMEM((chips, tr, rank), F32),
            pltpu.VMEM((chips, tr, rank), F32),
            pltpu.VMEM((chips, tok, wide), F32),
            pltpu.VMEM((chips, n_mp - 1, tq, wide), F32),
            pltpu.VMEM((chips, tq, wide), BF16),
            pltpu.VMEM((n_sub, tok, wide), BF16),
            dma((n_dp + 4,)),
        ]
        + pairs(chips) + pairs(many) + pairs(CHUNKS * n_mp) + pairs(CHUNKS * n_mp)
        + pairs(many) + pairs(many) + pairs(chips) + pairs(many) + pairs(many) + pairs(many)
        + pairs(PIECES * chips) + pairs(1) + pairs(chips * n_mp) + pairs(chips),
        compiler_params=pltpu.CompilerParams(
            collective_id=0, has_side_effects=True, vmem_limit_bytes=34 << 20
        ),
        cost_estimate=pl.CostEstimate(flops=64 * d * ff * rank, bytes_accessed=48 * d * ff, transcendentals=0),
        name="compress",
    )(*arguments)

    width, parts = min(512, ff), 4
    error_next, update, query_out, grad_out = pl.pallas_call(
        functools.partial(residual, n_dp, width),
        out_shape=(
            jax.ShapeDtypeStruct((d, ff), BF16),
            jax.ShapeDtypeStruct((pr, ff), F32),
            jax.ShapeDtypeStruct((ff, rank), F32),
            jax.ShapeDtypeStruct((tok, d // n_mp), BF16),
        ),
        in_specs=[vmem] * 5,
        out_specs=(hbm,) * 4,
        scratch_shapes=[
            pltpu.VMEM((ff // width, 3 * rank + tok, width), BF16),
            pltpu.VMEM((ff // width * parts, d // parts, width), BF16),
            pltpu.VMEM((ff // width, pr, width), F32),
            dma((ff // width * parts,)),
            dma((ff // width,)),
            dma((2,)),
        ],
        compiler_params=pltpu.CompilerParams(vmem_limit_bytes=26 << 20),
        cost_estimate=pl.CostEstimate(flops=8 * d * ff * rank, bytes_accessed=4 * d * ff, transcendentals=0),
        name="residual",
    )(error_held, hidden_held, query_next, factors, grad_input)
    return grad_out, error_next[None], update, query_out


def solution(mesh):
    n_dp, n_mp = mesh.shape["dp"], mesh.shape["mp"]
    in_specs = (P("dp", None), P("dp", "mp"), P("dp", "mp"), P("dp", None, "mp"), P("mp", None))
    out_specs = (P("dp", "mp"), P("dp", None, "mp"), P("dp", "mp"), P("mp", None))
    return jax.shard_map(
        functools.partial(local, n_dp, n_mp),
        mesh=mesh, in_specs=in_specs, out_specs=out_specs, check_vma=False,
    )
```

```python
import functools

import jax
import jax.numpy as jnp
from jax import lax
from jax.experimental import pallas as pl
from jax.experimental.pallas import tpu as pltpu
from jax.sharding import PartitionSpec as P

HIGHEST = lax.Precision.HIGHEST
MESH = pl.DeviceIdType.MESH
F32 = jnp.float32
BF16 = jnp.bfloat16
CORES = 2
PANEL = 16
PIECES = 2
CHUNKS = 2


def split(x):
    high = x.astype(BF16)
    return high, (x - high.astype(F32)).astype(BF16)


def dot(a, b, da=1, db=0, precision=None):
    return lax.dot_general(
        a, b, (((da,), (db,)), ((), ())), precision=precision, preferred_element_type=F32
    )


def halves(x):
    r = x.shape[1] // 2
    return x[:, :r] + x[:, r:]


def flip(v, r):
    out, bit = v, 1
    while bit <= r:
        if r & bit:
            out = out + bit - 2 * bit * lax.rem(v // bit, 2)
        bit *= 2
    return out


def bits_of(r):
    return [1 << b for b in range(r.bit_length()) if r >> b & 1]


def inverse_factor(gram, work):
    r = gram.shape[0]
    work[...] = gram
    prow = lax.broadcasted_iota(jnp.int32, (PANEL, r), 0)
    lane = lax.broadcasted_iota(jnp.int32, (PANEL, r), 1)
    rows = lax.broadcasted_iota(jnp.int32, (r, r), 0)
    cols = lax.broadcasted_iota(jnp.int32, (r, r), 1)
    for start in range(0, r, PANEL):
        panel = work[start : start + PANEL, :]
        spread = [
            jnp.broadcast_to(panel[:, start + k : start + k + 1], (PANEL, r)) for k in range(PANEL)
        ]
        for t in range(PANEL):
            scale = lax.rsqrt(spread[t][t : t + 1, :])
            below = jnp.where(prow > t, spread[t] * scale, 0.0)
            for k in range(t + 1, PANEL):
                spread[k] = spread[k] - below * (spread[k][t : t + 1, :] * scale)
            panel = jnp.where(lane == start + t, jnp.where(prow == t, 1.0, 0.0), panel)
            row = panel[t : t + 1, :] * scale
            panel = jnp.where(prow == t, row, panel - below * row)
        work[start : start + PANEL, :] = panel
        rest = start + PANEL
        for low, high in ((rest, rest + PANEL), (rest + PANEL, r)):
            if low < min(high, r):
                change = dot(panel[:, low:high], panel, 0, 0, HIGHEST)
                at = cols[low:high]
                old = jnp.where((at >= start) & (at < rest), 0.0, work[low:high, :])
                work[low:high, :] = old - change
    return jnp.where(cols <= rows, work[...], 0.0)


def compress(
    n_dp, n_mp, e_hbm, a_hbm, h_hbm, w_hbm, q_hbm, qn_ref, x_ref, g_ref, e, h,
    a, hall, w, q, q2, p, p2, pt2, tacc, aug, acc, zin, zfin, csend, crecv, xsend, xrecv,
    t, tcrecv, txsend, txrecv, part, zrecv, gsend, grecv,
    l_s, c_s, c_r, x_s, x_r, z_s, z_r, gz_s, gz_r, gx_s, gx_r, gc_s, gc_r,
    tc_s, tc_r, tx_s, tx_r, qx_s, qx_r, qc_s, qc_r, h_s, h_r, w_s, w_r, pz_s, pz_r, gg_s, gg_r,
):
    chips = n_dp // CORES
    me, mp = lax.axis_index("dp"), lax.axis_index("mp")
    chip, core = me // CORES, lax.rem(me, CORES)
    other = 1 - core
    partner = (chip * CORES + other, mp)
    d, rank = p.shape
    ff = t.shape[0]
    tok = a.shape[0]
    pr, tr, tq = d // n_dp, ff // n_dp, tok // n_mp
    wide = CORES * pr
    pc, tc = pr // CHUNKS, tr // CHUNKS
    zr = pc // n_mp if pc % (8 * n_mp) == 0 else pc
    n_sub = chips // n_mp
    goal = chip // n_sub

    def chip_at(r):
        return flip(chip, r)

    def same_core(r):
        return (chip_at(r) * CORES + core, mp)

    def along(r):
        return (me, flip(mp, r))

    def rows(i, n, unit=8):
        return pl.ds(pl.multiple_of(i * n, unit), n)

    def send(src, dst, s, r, to):
        return pltpu.make_async_remote_copy(
            src_ref=src, dst_ref=dst, send_sem=s, recv_sem=r, device_id=to, device_id_type=MESH
        )

    barrier = pltpu.get_barrier_semaphore()
    pl.semaphore_signal(barrier, inc=1, device_id=partner, device_id_type=MESH)
    for r in range(1, chips):
        pl.semaphore_signal(barrier, inc=1, device_id=same_core(r), device_id_type=MESH)
    for r in range(1, n_mp):
        pl.semaphore_signal(barrier, inc=1, device_id=along(r), device_id_type=MESH)
    for s in range(n_sub):
        for q_at in range(n_mp):
            source = mp * n_sub + s

            @pl.when(jnp.logical_or(source != chip, q_at != mp))
            def _():
                pl.semaphore_signal(
                    barrier, inc=1, device_id=(source * CORES + core, q_at), device_id_type=MESH
                )

    loads = []

    def load(src, dst):
        copy = pltpu.make_async_copy(src, dst, l_s.at[len(loads)])
        copy.start()
        loads.append(copy)
        return copy

    h_load = load(h_hbm, h)
    q_load = load(q_hbm, q)
    a_load = load(a_hbm, a)
    order = [chip_at(r) * CORES + other for r in range(1, chips)] + [partner[0]]
    order += [chip_at(r) * CORES + core for r in range(1, chips)] + [me]
    e_loads = [load(e_hbm.at[rows(b, pr, 16), :], e.at[rows(b, pr, 16), :]) for b in order]
    w_load = load(w_hbm, w.at[rows(core, pr, 16), :])

    pl.semaphore_wait(barrier, 1 + (chips - 1) + (n_mp - 1) + chips - jnp.where(goal == mp, 1, 0))

    tp = tok // PIECES
    h_copies = {}
    near = [r for r in range(1, chips) if len(bits_of(r)) == 1]
    pair = [r for r in range(1, chips) if len(bits_of(r)) == 2]
    many = [r for r in range(1, chips) if len(bits_of(r)) > 2]

    def send_hidden(r, k):
        at = pl.ds(k * tp, tp)
        i = r * PIECES + k
        copy = send(h_hbm.at[at, :], hall.at[r - 1, at, :], h_s.at[i], h_r.at[i], same_core(r))
        copy.start()
        h_copies[r, k] = copy

    def relay_hidden(r, k):
        via, to = bits_of(r) if k % 2 == 0 else bits_of(r)[::-1]
        at = pl.ds(k * tp, tp)
        i = r * PIECES + k
        copy = send(
            hall.at[via - 1, at, :], hall.at[r - 1, at, :], h_s.at[i], h_r.at[i], same_core(to)
        )
        copy.start()
        h_copies[r, k] = copy

    for r in near:
        send_hidden(r, 0)
    w_copy = send(w_hbm, w.at[rows(core, pr, 16), :], w_s.at[0], w_r.at[0], partner)
    w_copy.start()

    h_load.wait()
    q_load.wait()
    q_high, q_low = split(q[...])
    q2[:, :rank] = q_high
    q2[:, rank:] = q_low
    hq = halves(dot(h[...], q2[...]))
    hq2 = jnp.concatenate(split(hq), axis=1)
    a_load.wait()
    p[...] = halves(dot(a[...], hq2, 0, 0))

    def project(i):
        e_loads[i].wait()
        at = rows(order[i], pr, 16)
        return halves(dot(e[at, :], q2[...])) + p[at, :]

    core_copies = []
    for i in range(chips):
        csend[i] = project(i)
        copy = send(csend.at[i], crecv.at[i], c_s.at[i], c_r.at[i], partner)
        copy.start()
        core_copies.append(copy)
    x_copies = {}

    def send_chunk(i, k):
        at = pl.ds(k * pc, pc)
        n = i * CHUNKS + k
        copy = send(xsend.at[i, at, :], xrecv.at[i, at, :], x_s.at[n], x_r.at[n], same_core(i + 1))
        copy.start()
        x_copies[i, k] = copy

    for i in range(chips):
        value = project(chips + i)
        core_copies[i].wait_recv()
        xsend[i] = value + crecv[i]
        if i < chips - 1:
            send_chunk(i, 0)
    for k in range(1, CHUNKS):
        for i in range(chips - 1):
            send_chunk(i, k)

    z_parts = {}

    def partial_input(r):
        part[r] = dot(hall[r - 1] if r else h[...], w[...], 1, 1)

    def send_partial(r):
        for s in range(1, n_mp):
            i = r * n_mp + s
            copy = send(
                part.at[r, rows(flip(mp, s), tq), :], zrecv.at[r, s - 1],
                pz_s.at[i], pz_r.at[i], along(s),
            )
            copy.start()
            z_parts[r, s] = copy

    w_load.wait()
    w_copy.wait_recv()
    partial_input(0)

    def segment(k, i):
        return rows(i, zr) if zr < pc else pl.ds(0, pc)

    z_copies, gz = {}, {}
    for k in range(CHUNKS):
        at = pl.ds(k * pc, pc)
        value = xsend[chips - 1, at, :]
        for i in range(chips - 1):
            x_copies[i, k].wait_recv()
            value = value + xrecv[i, at, :]
        acc[k] = value
        for r in range(1, n_mp):
            n = k * n_mp + r
            copy = send(
                acc.at[k, segment(k, flip(mp, r)), :], zin.at[k, r], z_s.at[n], z_r.at[n], along(r)
            )
            copy.start()
            z_copies[r, k] = copy
    for r in near:
        for k in range(1, PIECES):
            send_hidden(r, k)
    for k in range(CHUNKS):
        value = acc[k, segment(k, mp), :]
        for r in range(1, n_mp):
            z_copies[r, k].wait_recv()
            value = value + zin[k, r]
        if zr < pc:
            zfin[k] = value
            here = pl.ds(pl.multiple_of(me * pr + k * pc + mp * zr, 8), zr)
            p[here, :] = value
            for r in range(1, n_mp):
                n = k * n_mp + r
                copy = send(zfin.at[k], p.at[here, :], gz_s.at[n], gz_r.at[n], along(r))
                copy.start()
                gz[r, k] = copy
        else:
            p[pl.ds(pl.multiple_of(me * pr + k * pc, 8), pc), :] = value

    class Gather:
        def __init__(self, ref, n, x_s, x_r, c_s, c_r):
            self.ref, self.n = ref, n
            self.x_s, self.x_r, self.c_s, self.c_r = x_s, x_r, c_s, c_r
            self.across, self.down = {}, {}

        def at(self, r, k):
            part = self.n // CHUNKS
            base = (chip_at(r) * CORES + core) * self.n + k * part
            return self.ref.at[pl.ds(pl.multiple_of(base, 8), part), :]

        def out(self, origin, r, k, to):
            block, n = self.at(origin, k), r * CHUNKS + k
            copy = send(block, block, self.x_s.at[n], self.x_r.at[n], same_core(to))
            copy.start()
            self.across[r, k] = copy

        def begin(self, k):
            for r in near + many:
                self.out(0, r, k, r)
            self.hand(0, k)

        def hand(self, r, k):
            block, n = self.at(r, k), r * CHUNKS + k
            copy = send(block, block, self.c_s.at[n], self.c_r.at[n], partner)
            copy.start()
            self.down[r, k] = copy

        def relay(self, r, k):
            self.across[r, k].wait_recv()
            for f in pair:
                via, to = bits_of(f) if k % 2 == 0 else bits_of(f)[::-1]
                if r == via:
                    self.out(r, f, k, to)
            self.hand(r, k)

        def wait(self, r):
            for k in range(CHUNKS):
                self.down[r, k].wait_recv()

        def finish(self):
            for copy in list(self.across.values()) + list(self.down.values()):
                copy.wait_send()

    gather = Gather(p, pr, gx_s, gx_r, gc_s, gc_r)
    for k in range(CHUNKS):
        if zr < pc:
            for r in range(1, n_mp):
                gz[r, k].wait_recv()
        gather.begin(k)
    send_partial(0)

    final = pair[-1]
    t_copies, tx_copies = [], {}

    def swap_term(i):
        block = chip_at((i + 1) % chips) * CORES + other
        copy = send(t.at[rows(block, tr), :], tcrecv.at[i], tc_s.at[i], tc_r.at[i], partner)
        copy.start()
        t_copies.append(copy)

    def send_term(i, k):
        at = pl.ds(k * tc, tc)
        n = i * CHUNKS + k
        copy = send(txsend.at[i, at, :], txrecv.at[i, at, :], tx_s.at[n], tx_r.at[n], same_core(i + 1))
        copy.start()
        tx_copies[i, k] = copy

    def sum_term(i):
        t_copies[i].wait_recv()
        txsend[i] = t[rows(chip_at((i + 1) % chips) * CORES + core, tr), :] + tcrecv[i]
        if i < chips - 1:
            send_term(i, 0)

    width = 256

    def accumulate(r, gram):
        gather.wait(r)
        at = pl.ds(pl.multiple_of(chip_at(r) * wide, 16), wide)
        block_rows = p[at, :]
        high, low = split(block_rows)
        p2[at, :rank] = high
        p2[at, rank:] = low
        turned = block_rows.T
        high, low = split(turned)
        pt2[:rank, :] = high
        pt2[rank:, :] = low
        last = r == final
        if last:
            ap = halves(dot(a[...], p2[...])).T
            ap2 = jnp.concatenate(split(ap), axis=0)

        def total(cols):
            both = dot(pt2[...], e[at, cols])
            value = both[:rank] + both[rank:]
            if r:
                value = value + tacc[:, cols]
            if last:
                both = dot(ap2, h[:, cols])
                value = (value + (both[:rank] + both[rank:])).T
            return value

        if last and tr % 128 == 0:
            for side in (other, core):
                for i in range(chips):
                    block = chip_at((i + 1) % chips) * CORES + side
                    cols = pl.ds(pl.multiple_of(block * tr, tr), tr)
                    t[rows(block, tr), :] = total(cols)
                if side is other:
                    for i in range(chips):
                        swap_term(i)
        else:
            for n in range(ff // width):
                cols = slice(n * width, (n + 1) * width)
                if last:
                    t[cols, :] = total(cols)
                else:
                    tacc[:, cols] = total(cols)
            if last:
                for i in range(chips):
                    swap_term(i)
        if last:
            for i in range(chips):
                sum_term(i)
        return lambda: gram + dot(turned, block_rows, 1, 0, HIGHEST)

    gram = accumulate(0, 0.0)()
    for r in near:
        gather.relay(r, 0)
    for r in near[:1]:
        for k in range(PIECES):
            h_copies[r, k].wait_recv()
        partial_input(r)
        send_partial(r)
    for k in range(1, CHUNKS):
        for r in near:
            gather.relay(r, k)
    for r in near[1:]:
        for k in range(PIECES):
            h_copies[r, k].wait_recv()
        partial_input(r)
        send_partial(r)
    for r in near:
        gram = accumulate(r, gram)()
    for r in many + pair[:-1]:
        for k in range(CHUNKS):
            gather.relay(r, k)
        gram = accumulate(r, gram)()
    for k in range(CHUNKS):
        gather.relay(final, k)
    for k in range(PIECES):
        for r in pair:
            relay_hidden(r, k)
        for r in many:
            send_hidden(r, k)
    add_gram = accumulate(final, gram)

    for k in range(1, CHUNKS):
        for i in range(chips - 1):
            send_term(i, k)
    inverse = inverse_factor(add_gram(), aug)
    for r in pair + many:
        for k in range(PIECES):
            h_copies[r, k].wait_recv()
        partial_input(r)
        send_partial(r)
    gather.finish()
    gather = Gather(qn_ref, tr, qx_s, qx_r, qc_s, qc_r)
    for k in range(CHUNKS):
        at = pl.ds(k * tc, tc)
        value = txsend[chips - 1, at, :]
        for i in range(chips - 1):
            tx_copies[i, k].wait_recv()
            value = value + txrecv[i, at, :]
        own = pl.ds(pl.multiple_of(me * tr + k * tc, 8), tc)
        qn_ref[own, :] = dot(value, inverse, 1, 1, HIGHEST) / n_dp
        gather.begin(k)
    for r in near:
        gather.relay(r, 0)
    high, low = split(dot(p[...], inverse, 1, 1, HIGHEST))
    x_ref[:, :rank] = high
    x_ref[:, rank : 2 * rank] = low
    x_ref[:, 2 * rank : 3 * rank] = high
    x_ref[:, 3 * rank :] = a[...].T
    for k in range(1, CHUNKS):
        for r in near:
            gather.relay(r, k)

    g_copies = []
    for r in range(chips):
        value = part[r, rows(mp, tq), :]
        for s in range(1, n_mp):
            z_parts[r, s].wait_recv()
            value = value + zrecv[r, s - 1]
        gsend[r] = value.astype(BF16)
        place = grecv.at[lax.rem(chip, n_sub), rows(mp, tq, 16), :]
        slot = lax.rem(chip, n_sub) * n_mp + mp
        to = (chip_at(r) * CORES + core, goal)
        copy = send(gsend.at[r], place, gg_s.at[r], gg_r.at[slot], to)
        if r:
            copy.start()
        else:

            @pl.when(goal != mp)
            def _():
                copy.start()

            @pl.when(goal == mp)
            def _():
                place[...] = gsend[0]

        g_copies.append(copy)

    for r in pair + many:
        for k in range(CHUNKS):
            gather.relay(r, k)
    for s in range(n_sub):
        for q_at in range(n_mp):
            at = pl.ds(q_at * tq, tq)
            arrival = send(
                gsend.at[0], grecv.at[s, at, :], gg_s.at[0], gg_r.at[s * n_mp + q_at], partner
            )

            @pl.when(jnp.logical_or(mp * n_sub + s != chip, q_at != mp))
            def _():
                arrival.wait_recv()

        g_ref[:, s * wide : (s + 1) * wide] = grecv[s]
    for r in range(chips):
        gather.wait(r)
    gather.finish()
    started = [w_copy] + core_copies + t_copies
    for copies in (x_copies, z_copies, gz, tx_copies, h_copies, z_parts):
        started += list(copies.values())
    for copy in started:
        copy.wait_send()
    for r in range(1, chips):
        g_copies[r].wait_send()

    @pl.when(goal != mp)
    def _():
        g_copies[0].wait_send()


def residual(
    n_dp, width, e_ref, h_ref, qn_ref, x_ref, g_ref, out_hbm, up_hbm, q_hbm, g_hbm,
    y, out, up, o_s, u_s, k_s,
):
    d, ff = e_ref.shape
    rank = qn_ref.shape[1]
    share = up_hbm.shape[0]
    parts = d // out.shape[1]
    block = out.shape[1]
    copies = []

    def store(src, dst, sem):
        copy = pltpu.make_async_copy(src, dst, sem)
        copy.start()
        copies.append(copy)

    store(qn_ref, q_hbm, k_s.at[0])
    store(g_ref, g_hbm, k_s.at[1])
    own = pl.ds(pl.multiple_of(lax.axis_index("dp") * share, 16), share)
    for j in range(ff // width):
        cols = slice(j * width, (j + 1) * width)
        high, low = split(-qn_ref[cols, :].T)
        y[j, :rank] = high
        y[j, rank : 2 * rank] = high
        y[j, 2 * rank : 3 * rank] = low
        y[j, 3 * rank :] = h_ref[:, cols]
        up[j] = -dot(x_ref[own, : 3 * rank], y[j, : 3 * rank])
        store(up.at[j], up_hbm.at[:, cols], u_s.at[j])
        for i in range(parts):
            at = slice(i * block, (i + 1) * block)
            n = j * parts + i
            out[n] = (e_ref[at, cols].astype(F32) + dot(x_ref[at, :], y[j])).astype(BF16)
            store(out.at[n], out_hbm.at[at, cols], o_s.at[n])
    for copy in copies:
        copy.wait()


def local(n_dp, n_mp, activations, grad_hidden, up_weight, error_feedback, query_previous):
    error = error_feedback[0]
    d, ff = error.shape
    tok, rank = activations.shape[0], query_previous.shape[1]
    chips = n_dp // CORES
    pr, tr, tq = d // n_dp, ff // n_dp, tok // n_mp
    wide = CORES * pr
    pc = pr // CHUNKS
    zr = pc // n_mp if pc % (8 * n_mp) == 0 else pc
    n_sub = chips // n_mp
    many = CHUNKS * chips
    vmem = pl.BlockSpec(memory_space=pltpu.VMEM)
    hbm = pl.BlockSpec(memory_space=pl.ANY)
    dma = pltpu.SemaphoreType.DMA
    pairs = lambda n: [dma((n,)), dma((n,))]
    arguments = [
        pltpu.with_memory_space_constraint(x, pltpu.HBM)
        for x in (error, activations, grad_hidden, up_weight, query_previous)
    ]
    query_next, factors, grad_input, error_held, hidden_held = pl.pallas_call(
        functools.partial(compress, n_dp, n_mp),
        out_shape=(
            pltpu.VMEM((ff, rank), F32),
            pltpu.VMEM((d, 3 * rank + tok), BF16),
            pltpu.VMEM((tok, d // n_mp), BF16),
            pltpu.VMEM((d, ff), BF16),
            pltpu.VMEM((tok, ff), BF16),
        ),
        in_specs=[hbm] * 5,
        out_specs=(vmem,) * 5,
        scratch_shapes=[
            pltpu.VMEM((tok, d), BF16),
            pltpu.VMEM((chips - 1, tok, ff), BF16),
            pltpu.VMEM((wide, ff), BF16),
            pltpu.VMEM((ff, rank), F32),
            pltpu.VMEM((ff, 2 * rank), BF16),
            pltpu.VMEM((d, rank), F32),
            pltpu.VMEM((d, 2 * rank), BF16),
            pltpu.VMEM((2 * rank, wide), BF16),
            pltpu.VMEM((rank, ff), F32),
            pltpu.VMEM((rank, rank), F32),
            pltpu.VMEM((CHUNKS, pc, rank), F32),
            pltpu.VMEM((CHUNKS, n_mp, zr, rank), F32),
            pltpu.VMEM((CHUNKS, zr, rank), F32),
            pltpu.VMEM((chips, pr, rank), F32),
            pltpu.VMEM((chips, pr, rank), F32),
            pltpu.VMEM((chips, pr, rank), F32),
            pltpu.VMEM((chips, pr, rank), F32),
            pltpu.VMEM((ff, rank), F32),
            pltpu.VMEM((chips, tr, rank), F32),
            pltpu.VMEM((chips, tr, rank), F32),
            pltpu.VMEM((chips, tr, rank), F32),
            pltpu.VMEM((chips, tok, wide), F32),
            pltpu.VMEM((chips, n_mp - 1, tq, wide), F32),
            pltpu.VMEM((chips, tq, wide), BF16),
            pltpu.VMEM((n_sub, tok, wide), BF16),
            dma((n_dp + 4,)),
        ]
        + pairs(chips) + pairs(many) + pairs(CHUNKS * n_mp) + pairs(CHUNKS * n_mp)
        + pairs(many) + pairs(many) + pairs(chips) + pairs(many) + pairs(many) + pairs(many)
        + pairs(PIECES * chips) + pairs(1) + pairs(chips * n_mp) + pairs(chips),
        compiler_params=pltpu.CompilerParams(
            collective_id=0, has_side_effects=True, vmem_limit_bytes=34 << 20
        ),
        cost_estimate=pl.CostEstimate(flops=64 * d * ff * rank, bytes_accessed=48 * d * ff, transcendentals=0),
        name="compress",
    )(*arguments)

    width, parts = min(512, ff), 4
    error_next, update, query_out, grad_out = pl.pallas_call(
        functools.partial(residual, n_dp, width),
        out_shape=(
            jax.ShapeDtypeStruct((d, ff), BF16),
            jax.ShapeDtypeStruct((pr, ff), F32),
            jax.ShapeDtypeStruct((ff, rank), F32),
            jax.ShapeDtypeStruct((tok, d // n_mp), BF16),
        ),
        in_specs=[vmem] * 5,
        out_specs=(hbm,) * 4,
        scratch_shapes=[
            pltpu.VMEM((ff // width, 3 * rank + tok, width), BF16),
            pltpu.VMEM((ff // width * parts, d // parts, width), BF16),
            pltpu.VMEM((ff // width, pr, width), F32),
            dma((ff // width * parts,)),
            dma((ff // width,)),
            dma((2,)),
        ],
        compiler_params=pltpu.CompilerParams(vmem_limit_bytes=26 << 20),
        cost_estimate=pl.CostEstimate(flops=8 * d * ff * rank, bytes_accessed=4 * d * ff, transcendentals=0),
        name="residual",
    )(error_held, hidden_held, query_next, factors, grad_input)
    return grad_out, error_next[None], update, query_out


def solution(mesh):
    n_dp, n_mp = mesh.shape["dp"], mesh.shape["mp"]
    in_specs = (P("dp", None), P("dp", "mp"), P("dp", "mp"), P("dp", None, "mp"), P("mp", None))
    out_specs = (P("dp", "mp"), P("dp", None, "mp"), P("dp", "mp"), P("mp", None))
    return jax.shard_map(
        functools.partial(local, n_dp, n_mp),
        mesh=mesh, in_specs=in_specs, out_specs=out_specs, check_vma=False,
    )
```

```python
import functools

import jax
import jax.numpy as jnp
from jax import lax
from jax.experimental import pallas as pl
from jax.experimental.pallas import tpu as pltpu
from jax.sharding import PartitionSpec as P

HIGHEST = lax.Precision.HIGHEST
MESH = pl.DeviceIdType.MESH
F32 = jnp.float32
BF16 = jnp.bfloat16
CORES = 2
PANEL = 16
PIECES = 2
CHUNKS = 2


def split(x):
    high = x.astype(BF16)
    return high, (x - high.astype(F32)).astype(BF16)


def dot(a, b, da=1, db=0, precision=None):
    return lax.dot_general(
        a, b, (((da,), (db,)), ((), ())), precision=precision, preferred_element_type=F32
    )


def halves(x):
    r = x.shape[1] // 2
    return x[:, :r] + x[:, r:]


def flip(v, r):
    out, bit = v, 1
    while bit <= r:
        if r & bit:
            out = out + bit - 2 * bit * lax.rem(v // bit, 2)
        bit *= 2
    return out


def bits_of(r):
    return [1 << b for b in range(r.bit_length()) if r >> b & 1]


def inverse_factor(gram, work):
    r = gram.shape[0]
    work[...] = gram
    prow = lax.broadcasted_iota(jnp.int32, (PANEL, r), 0)
    lane = lax.broadcasted_iota(jnp.int32, (PANEL, r), 1)
    rows = lax.broadcasted_iota(jnp.int32, (r, r), 0)
    cols = lax.broadcasted_iota(jnp.int32, (r, r), 1)
    for start in range(0, r, PANEL):
        panel = work[start : start + PANEL, :]
        spread = [
            jnp.broadcast_to(panel[:, start + k : start + k + 1], (PANEL, r)) for k in range(PANEL)
        ]
        for t in range(PANEL):
            scale = lax.rsqrt(spread[t][t : t + 1, :])
            below = jnp.where(prow > t, spread[t] * scale, 0.0)
            for k in range(t + 1, PANEL):
                spread[k] = spread[k] - below * (spread[k][t : t + 1, :] * scale)
            panel = jnp.where(lane == start + t, jnp.where(prow == t, 1.0, 0.0), panel)
            row = panel[t : t + 1, :] * scale
            panel = jnp.where(prow == t, row, panel - below * row)
        work[start : start + PANEL, :] = panel
        rest = start + PANEL
        for low, high in ((rest, rest + PANEL), (rest + PANEL, r)):
            if low < min(high, r):
                change = dot(panel[:, low:high], panel, 0, 0, HIGHEST)
                at = cols[low:high]
                old = jnp.where((at >= start) & (at < rest), 0.0, work[low:high, :])
                work[low:high, :] = old - change
    return jnp.where(cols <= rows, work[...], 0.0)


def compress(
    n_dp, n_mp, e_hbm, a_hbm, h_hbm, w_hbm, q_hbm, qn_ref, x_ref, g_ref, e, h,
    a, hall, w, q, q2, p, p2, pt2, tacc, aug, acc, zin, zfin, csend, crecv, xsend, xrecv,
    t, tcrecv, txsend, txrecv, part, zrecv, gsend, grecv,
    l_s, c_s, c_r, x_s, x_r, z_s, z_r, gz_s, gz_r, gx_s, gx_r, gc_s, gc_r,
    tc_s, tc_r, tx_s, tx_r, qx_s, qx_r, qc_s, qc_r, h_s, h_r, w_s, w_r, pz_s, pz_r, gg_s, gg_r,
):
    chips = n_dp // CORES
    me, mp = lax.axis_index("dp"), lax.axis_index("mp")
    chip, core = me // CORES, lax.rem(me, CORES)
    other = 1 - core
    partner = (chip * CORES + other, mp)
    d, rank = p.shape
    ff = t.shape[0]
    tok = a.shape[0]
    pr, tr, tq = d // n_dp, ff // n_dp, tok // n_mp
    wide = CORES * pr
    pc, tc = pr // CHUNKS, tr // CHUNKS
    zr = pc // n_mp if pc % (8 * n_mp) == 0 else pc
    n_sub = chips // n_mp
    goal = chip // n_sub

    def chip_at(r):
        return flip(chip, r)

    def same_core(r):
        return (chip_at(r) * CORES + core, mp)

    def along(r):
        return (me, flip(mp, r))

    def rows(i, n, unit=8):
        return pl.ds(pl.multiple_of(i * n, unit), n)

    def send(src, dst, s, r, to):
        return pltpu.make_async_remote_copy(
            src_ref=src, dst_ref=dst, send_sem=s, recv_sem=r, device_id=to, device_id_type=MESH
        )

    barrier = pltpu.get_barrier_semaphore()
    pl.semaphore_signal(barrier, inc=1, device_id=partner, device_id_type=MESH)
    for r in range(1, chips):
        pl.semaphore_signal(barrier, inc=1, device_id=same_core(r), device_id_type=MESH)
    for r in range(1, n_mp):
        pl.semaphore_signal(barrier, inc=1, device_id=along(r), device_id_type=MESH)
    for s in range(n_sub):
        for q_at in range(n_mp):
            source = mp * n_sub + s

            @pl.when(jnp.logical_or(source != chip, q_at != mp))
            def _():
                pl.semaphore_signal(
                    barrier, inc=1, device_id=(source * CORES + core, q_at), device_id_type=MESH
                )

    loads = []

    def load(src, dst):
        copy = pltpu.make_async_copy(src, dst, l_s.at[len(loads)])
        copy.start()
        loads.append(copy)
        return copy

    q_load = load(q_hbm, q)
    h_load = load(h_hbm, h)
    a_load = load(a_hbm, a)
    order = [chip_at(r) * CORES + other for r in range(1, chips)] + [partner[0]]
    order += [chip_at(r) * CORES + core for r in range(1, chips)] + [me]
    e_loads = [load(e_hbm.at[rows(b, pr, 16), :], e.at[rows(b, pr, 16), :]) for b in order]
    w_load = load(w_hbm, w.at[rows(core, pr, 16), :])

    pl.semaphore_wait(barrier, 1 + (chips - 1) + (n_mp - 1) + chips - jnp.where(goal == mp, 1, 0))

    tp = tok // PIECES
    h_copies = {}
    near = [r for r in range(1, chips) if len(bits_of(r)) == 1]
    pair = [r for r in range(1, chips) if len(bits_of(r)) == 2]
    many = [r for r in range(1, chips) if len(bits_of(r)) > 2]

    def send_hidden(r, k):
        at = pl.ds(k * tp, tp)
        i = r * PIECES + k
        copy = send(h_hbm.at[at, :], hall.at[r - 1, at, :], h_s.at[i], h_r.at[i], same_core(r))
        copy.start()
        h_copies[r, k] = copy

    def relay_hidden(r, k):
        via, to = bits_of(r) if k % 2 == 0 else bits_of(r)[::-1]
        at = pl.ds(k * tp, tp)
        i = r * PIECES + k
        copy = send(
            hall.at[via - 1, at, :], hall.at[r - 1, at, :], h_s.at[i], h_r.at[i], same_core(to)
        )
        copy.start()
        h_copies[r, k] = copy

    for r in near:
        send_hidden(r, 0)
    w_copy = send(w_hbm, w.at[rows(core, pr, 16), :], w_s.at[0], w_r.at[0], partner)
    w_copy.start()

    q_load.wait()
    q_high, q_low = split(q[...])
    q2[:, :rank] = q_high
    q2[:, rank:] = q_low
    h_load.wait()
    hq = halves(dot(h[...], q2[...]))
    hq2 = jnp.concatenate(split(hq), axis=1)
    a_load.wait()
    p[...] = halves(dot(a[...], hq2, 0, 0))

    def project(i):
        e_loads[i].wait()
        at = rows(order[i], pr, 16)
        return halves(dot(e[at, :], q2[...])) + p[at, :]

    core_copies = []
    for i in range(chips):
        csend[i] = project(i)
        copy = send(csend.at[i], crecv.at[i], c_s.at[i], c_r.at[i], partner)
        copy.start()
        core_copies.append(copy)
    x_copies = {}

    def send_chunk(i, k):
        at = pl.ds(k * pc, pc)
        n = i * CHUNKS + k
        copy = send(xsend.at[i, at, :], xrecv.at[i, at, :], x_s.at[n], x_r.at[n], same_core(i + 1))
        copy.start()
        x_copies[i, k] = copy

    for i in range(chips):
        value = project(chips + i)
        core_copies[i].wait_recv()
        xsend[i] = value + crecv[i]
        if i < chips - 1:
            send_chunk(i, 0)
    for k in range(1, CHUNKS):
        for i in range(chips - 1):
            send_chunk(i, k)

    z_parts = {}

    def partial_input(r):
        part[r] = dot(hall[r - 1] if r else h[...], w[...], 1, 1)

    def send_partial(r):
        for s in range(1, n_mp):
            i = r * n_mp + s
            copy = send(
                part.at[r, rows(flip(mp, s), tq), :], zrecv.at[r, s - 1],
                pz_s.at[i], pz_r.at[i], along(s),
            )
            copy.start()
            z_parts[r, s] = copy

    w_load.wait()
    w_copy.wait_recv()
    partial_input(0)
    x_ref[:, 3 * rank :] = a[...].T

    def segment(k, i):
        return rows(i, zr) if zr < pc else pl.ds(0, pc)

    z_copies, gz = {}, {}
    for k in range(CHUNKS):
        at = pl.ds(k * pc, pc)
        value = xsend[chips - 1, at, :]
        for i in range(chips - 1):
            x_copies[i, k].wait_recv()
            value = value + xrecv[i, at, :]
        acc[k] = value
        for r in range(1, n_mp):
            n = k * n_mp + r
            copy = send(
                acc.at[k, segment(k, flip(mp, r)), :], zin.at[k, r], z_s.at[n], z_r.at[n], along(r)
            )
            copy.start()
            z_copies[r, k] = copy
    for r in near:
        for k in range(1, PIECES):
            send_hidden(r, k)
    for k in range(CHUNKS):
        value = acc[k, segment(k, mp), :]
        for r in range(1, n_mp):
            z_copies[r, k].wait_recv()
            value = value + zin[k, r]
        if zr < pc:
            zfin[k] = value
            here = pl.ds(pl.multiple_of(me * pr + k * pc + mp * zr, 8), zr)
            p[here, :] = value
            for r in range(1, n_mp):
                n = k * n_mp + r
                copy = send(zfin.at[k], p.at[here, :], gz_s.at[n], gz_r.at[n], along(r))
                copy.start()
                gz[r, k] = copy
        else:
            p[pl.ds(pl.multiple_of(me * pr + k * pc, 8), pc), :] = value

    class Gather:
        def __init__(self, ref, n, x_s, x_r, c_s, c_r):
            self.ref, self.n = ref, n
            self.x_s, self.x_r, self.c_s, self.c_r = x_s, x_r, c_s, c_r
            self.across, self.down = {}, {}

        def at(self, r, k):
            part = self.n // CHUNKS
            base = (chip_at(r) * CORES + core) * self.n + k * part
            return self.ref.at[pl.ds(pl.multiple_of(base, 8), part), :]

        def out(self, origin, r, k, to):
            block, n = self.at(origin, k), r * CHUNKS + k
            copy = send(block, block, self.x_s.at[n], self.x_r.at[n], same_core(to))
            copy.start()
            self.across[r, k] = copy

        def begin(self, k):
            for r in near + many:
                self.out(0, r, k, r)
            self.hand(0, k)

        def hand(self, r, k):
            block, n = self.at(r, k), r * CHUNKS + k
            copy = send(block, block, self.c_s.at[n], self.c_r.at[n], partner)
            copy.start()
            self.down[r, k] = copy

        def relay(self, r, k):
            self.across[r, k].wait_recv()
            for f in pair:
                via, to = bits_of(f) if k % 2 == 0 else bits_of(f)[::-1]
                if r == via:
                    self.out(r, f, k, to)
            self.hand(r, k)

        def wait(self, r):
            for k in range(CHUNKS):
                self.down[r, k].wait_recv()

        def finish(self):
            for copy in list(self.across.values()) + list(self.down.values()):
                copy.wait_send()

    gather = Gather(p, pr, gx_s, gx_r, gc_s, gc_r)
    for k in range(CHUNKS):
        if zr < pc:
            for r in range(1, n_mp):
                gz[r, k].wait_recv()
        gather.begin(k)
    send_partial(0)

    final = pair[-1]
    t_copies, tx_copies = [], {}

    def swap_term(i):
        block = chip_at((i + 1) % chips) * CORES + other
        copy = send(t.at[rows(block, tr), :], tcrecv.at[i], tc_s.at[i], tc_r.at[i], partner)
        copy.start()
        t_copies.append(copy)

    def send_term(i, k):
        at = pl.ds(k * tc, tc)
        n = i * CHUNKS + k
        copy = send(txsend.at[i, at, :], txrecv.at[i, at, :], tx_s.at[n], tx_r.at[n], same_core(i + 1))
        copy.start()
        tx_copies[i, k] = copy

    def sum_term(i):
        t_copies[i].wait_recv()
        txsend[i] = t[rows(chip_at((i + 1) % chips) * CORES + core, tr), :] + tcrecv[i]
        if i < chips - 1:
            send_term(i, 0)

    width = 256

    def accumulate(r, gram):
        gather.wait(r)
        at = pl.ds(pl.multiple_of(chip_at(r) * wide, 16), wide)
        block_rows = p[at, :]
        high, low = split(block_rows)
        p2[at, :rank] = high
        p2[at, rank:] = low
        turned = block_rows.T
        high, low = split(turned)
        pt2[:rank, :] = high
        pt2[rank:, :] = low
        last = r == final
        if last:
            ap = halves(dot(a[...], p2[...])).T
            ap2 = jnp.concatenate(split(ap), axis=0)

        def total(cols):
            both = dot(pt2[...], e[at, cols])
            value = both[:rank] + both[rank:]
            if r:
                value = value + tacc[:, cols]
            if last:
                both = dot(ap2, h[:, cols])
                value = (value + (both[:rank] + both[rank:])).T
            return value

        if last and tr % 128 == 0:
            for side in (other, core):
                for i in range(chips):
                    block = chip_at((i + 1) % chips) * CORES + side
                    cols = pl.ds(pl.multiple_of(block * tr, tr), tr)
                    t[rows(block, tr), :] = total(cols)
                if side is other:
                    for i in range(chips):
                        swap_term(i)
        else:
            for n in range(ff // width):
                cols = slice(n * width, (n + 1) * width)
                if last:
                    t[cols, :] = total(cols)
                else:
                    tacc[:, cols] = total(cols)
            if last:
                for i in range(chips):
                    swap_term(i)
        if last:
            for i in range(chips):
                sum_term(i)
        return lambda: gram + dot(turned, block_rows, 1, 0, HIGHEST)

    gram = accumulate(0, 0.0)()
    for r in near:
        gather.relay(r, 0)
    for r in near[:1]:
        for k in range(PIECES):
            h_copies[r, k].wait_recv()
        partial_input(r)
        send_partial(r)
    for k in range(1, CHUNKS):
        for r in near:
            gather.relay(r, k)
    for r in near[1:]:
        for k in range(PIECES):
            h_copies[r, k].wait_recv()
        partial_input(r)
        send_partial(r)
    for r in near:
        gram = accumulate(r, gram)()
    for r in many + pair[:-1]:
        for k in range(CHUNKS):
            gather.relay(r, k)
        gram = accumulate(r, gram)()
    for k in range(CHUNKS):
        gather.relay(final, k)
    for k in range(PIECES):
        for r in pair:
            relay_hidden(r, k)
        for r in many:
            send_hidden(r, k)
    add_gram = accumulate(final, gram)

    for k in range(1, CHUNKS):
        for i in range(chips - 1):
            send_term(i, k)
    inverse = inverse_factor(add_gram(), aug)
    for r in pair + many:
        for k in range(PIECES):
            h_copies[r, k].wait_recv()
        partial_input(r)
        send_partial(r)
    high, low = split(dot(p[...], inverse, 1, 1, HIGHEST))
    x_ref[:, :rank] = high
    x_ref[:, rank : 2 * rank] = low
    x_ref[:, 2 * rank : 3 * rank] = high
    gather.finish()
    gather = Gather(qn_ref, tr, qx_s, qx_r, qc_s, qc_r)
    for k in range(CHUNKS):
        at = pl.ds(k * tc, tc)
        value = txsend[chips - 1, at, :]
        for i in range(chips - 1):
            tx_copies[i, k].wait_recv()
            value = value + txrecv[i, at, :]
        own = pl.ds(pl.multiple_of(me * tr + k * tc, 8), tc)
        qn_ref[own, :] = dot(value, inverse, 1, 1, HIGHEST) / n_dp
        gather.begin(k)
    for r in near:
        gather.relay(r, 0)
    for k in range(1, CHUNKS):
        for r in near:
            gather.relay(r, k)

    g_copies = []
    for r in range(chips):
        value = part[r, rows(mp, tq), :]
        for s in range(1, n_mp):
            z_parts[r, s].wait_recv()
            value = value + zrecv[r, s - 1]
        gsend[r] = value.astype(BF16)
        place = grecv.at[lax.rem(chip, n_sub), rows(mp, tq, 16), :]
        slot = lax.rem(chip, n_sub) * n_mp + mp
        to = (chip_at(r) * CORES + core, goal)
        copy = send(gsend.at[r], place, gg_s.at[r], gg_r.at[slot], to)
        if r:
            copy.start()
        else:

            @pl.when(goal != mp)
            def _():
                copy.start()

            @pl.when(goal == mp)
            def _():
                place[...] = gsend[0]

        g_copies.append(copy)

    for r in pair + many:
        for k in range(CHUNKS):
            gather.relay(r, k)
    for s in range(n_sub):
        for q_at in range(n_mp):
            at = pl.ds(q_at * tq, tq)
            arrival = send(
                gsend.at[0], grecv.at[s, at, :], gg_s.at[0], gg_r.at[s * n_mp + q_at], partner
            )

            @pl.when(jnp.logical_or(mp * n_sub + s != chip, q_at != mp))
            def _():
                arrival.wait_recv()

        g_ref[:, s * wide : (s + 1) * wide] = grecv[s]
    for r in range(chips):
        gather.wait(r)
    gather.finish()
    started = [w_copy] + core_copies + t_copies
    for copies in (x_copies, z_copies, gz, tx_copies, h_copies, z_parts):
        started += list(copies.values())
    for copy in started:
        copy.wait_send()
    for r in range(1, chips):
        g_copies[r].wait_send()

    @pl.when(goal != mp)
    def _():
        g_copies[0].wait_send()


def residual(
    n_dp, width, e_ref, h_ref, qn_ref, x_ref, g_ref, out_hbm, up_hbm, q_hbm, g_hbm,
    y, out, up, o_s, u_s, k_s,
):
    d, ff = e_ref.shape
    rank = qn_ref.shape[1]
    share = up_hbm.shape[0]
    parts = d // out.shape[1]
    block = out.shape[1]
    copies = []

    def store(src, dst, sem):
        copy = pltpu.make_async_copy(src, dst, sem)
        copy.start()
        copies.append(copy)

    store(qn_ref, q_hbm, k_s.at[0])
    store(g_ref, g_hbm, k_s.at[1])
    own = pl.ds(pl.multiple_of(lax.axis_index("dp") * share, 16), share)
    for j in range(ff // width):
        cols = slice(j * width, (j + 1) * width)
        high, low = split(-qn_ref[cols, :].T)
        y[j, :rank] = high
        y[j, rank : 2 * rank] = high
        y[j, 2 * rank : 3 * rank] = low
        y[j, 3 * rank :] = h_ref[:, cols]
        up[j] = -dot(x_ref[own, : 3 * rank], y[j, : 3 * rank])
        store(up.at[j], up_hbm.at[:, cols], u_s.at[j])
        for i in range(parts):
            at = slice(i * block, (i + 1) * block)
            n = j * parts + i
            out[n] = (e_ref[at, cols].astype(F32) + dot(x_ref[at, :], y[j])).astype(BF16)
            store(out.at[n], out_hbm.at[at, cols], o_s.at[n])
    for copy in copies:
        copy.wait()


def local(n_dp, n_mp, activations, grad_hidden, up_weight, error_feedback, query_previous):
    error = error_feedback[0]
    d, ff = error.shape
    tok, rank = activations.shape[0], query_previous.shape[1]
    chips = n_dp // CORES
    pr, tr, tq = d // n_dp, ff // n_dp, tok // n_mp
    wide = CORES * pr
    pc = pr // CHUNKS
    zr = pc // n_mp if pc % (8 * n_mp) == 0 else pc
    n_sub = chips // n_mp
    many = CHUNKS * chips
    vmem = pl.BlockSpec(memory_space=pltpu.VMEM)
    hbm = pl.BlockSpec(memory_space=pl.ANY)
    dma = pltpu.SemaphoreType.DMA
    pairs = lambda n: [dma((n,)), dma((n,))]
    arguments = [
        pltpu.with_memory_space_constraint(x, pltpu.HBM)
        for x in (error, activations, grad_hidden, up_weight, query_previous)
    ]
    query_next, factors, grad_input, error_held, hidden_held = pl.pallas_call(
        functools.partial(compress, n_dp, n_mp),
        out_shape=(
            pltpu.VMEM((ff, rank), F32),
            pltpu.VMEM((d, 3 * rank + tok), BF16),
            pltpu.VMEM((tok, d // n_mp), BF16),
            pltpu.VMEM((d, ff), BF16),
            pltpu.VMEM((tok, ff), BF16),
        ),
        in_specs=[hbm] * 5,
        out_specs=(vmem,) * 5,
        scratch_shapes=[
            pltpu.VMEM((tok, d), BF16),
            pltpu.VMEM((chips - 1, tok, ff), BF16),
            pltpu.VMEM((wide, ff), BF16),
            pltpu.VMEM((ff, rank), F32),
            pltpu.VMEM((ff, 2 * rank), BF16),
            pltpu.VMEM((d, rank), F32),
            pltpu.VMEM((d, 2 * rank), BF16),
            pltpu.VMEM((2 * rank, wide), BF16),
            pltpu.VMEM((rank, ff), F32),
            pltpu.VMEM((rank, rank), F32),
            pltpu.VMEM((CHUNKS, pc, rank), F32),
            pltpu.VMEM((CHUNKS, n_mp, zr, rank), F32),
            pltpu.VMEM((CHUNKS, zr, rank), F32),
            pltpu.VMEM((chips, pr, rank), F32),
            pltpu.VMEM((chips, pr, rank), F32),
            pltpu.VMEM((chips, pr, rank), F32),
            pltpu.VMEM((chips, pr, rank), F32),
            pltpu.VMEM((ff, rank), F32),
            pltpu.VMEM((chips, tr, rank), F32),
            pltpu.VMEM((chips, tr, rank), F32),
            pltpu.VMEM((chips, tr, rank), F32),
            pltpu.VMEM((chips, tok, wide), F32),
            pltpu.VMEM((chips, n_mp - 1, tq, wide), F32),
            pltpu.VMEM((chips, tq, wide), BF16),
            pltpu.VMEM((n_sub, tok, wide), BF16),
            dma((n_dp + 4,)),
        ]
        + pairs(chips) + pairs(many) + pairs(CHUNKS * n_mp) + pairs(CHUNKS * n_mp)
        + pairs(many) + pairs(many) + pairs(chips) + pairs(many) + pairs(many) + pairs(many)
        + pairs(PIECES * chips) + pairs(1) + pairs(chips * n_mp) + pairs(chips),
        compiler_params=pltpu.CompilerParams(
            collective_id=0, has_side_effects=True, vmem_limit_bytes=34 << 20
        ),
        cost_estimate=pl.CostEstimate(flops=64 * d * ff * rank, bytes_accessed=48 * d * ff, transcendentals=0),
        name="compress",
    )(*arguments)

    width, parts = min(512, ff), 4
    error_next, update, query_out, grad_out = pl.pallas_call(
        functools.partial(residual, n_dp, width),
        out_shape=(
            jax.ShapeDtypeStruct((d, ff), BF16),
            jax.ShapeDtypeStruct((pr, ff), F32),
            jax.ShapeDtypeStruct((ff, rank), F32),
            jax.ShapeDtypeStruct((tok, d // n_mp), BF16),
        ),
        in_specs=[vmem] * 5,
        out_specs=(hbm,) * 4,
        scratch_shapes=[
            pltpu.VMEM((ff // width, 3 * rank + tok, width), BF16),
            pltpu.VMEM((ff // width * parts, d // parts, width), BF16),
            pltpu.VMEM((ff // width, pr, width), F32),
            dma((ff // width * parts,)),
            dma((ff // width,)),
            dma((2,)),
        ],
        compiler_params=pltpu.CompilerParams(vmem_limit_bytes=26 << 20),
        cost_estimate=pl.CostEstimate(flops=8 * d * ff * rank, bytes_accessed=4 * d * ff, transcendentals=0),
        name="residual",
    )(error_held, hidden_held, query_next, factors, grad_input)
    return grad_out, error_next[None], update, query_out


def solution(mesh):
    n_dp, n_mp = mesh.shape["dp"], mesh.shape["mp"]
    in_specs = (P("dp", None), P("dp", "mp"), P("dp", "mp"), P("dp", None, "mp"), P("mp", None))
    out_specs = (P("dp", "mp"), P("dp", None, "mp"), P("dp", "mp"), P("mp", None))
    return jax.shard_map(
        functools.partial(local, n_dp, n_mp),
        mesh=mesh, in_specs=in_specs, out_specs=out_specs, check_vma=False,
    )
```
